32 devices in a mesh: groups: 2 (over y), space: 4 (over z), inst: 2 (over x), row: 2 (over core).
Axes of the slice: x: 2, y: 2, z: 4, core: 2. Of those that a mesh axis runs over, the one named last changes fastest.
Arguments:
- solution: bfloat16 [2, 4, 320, 8192], P('row', 'inst', None, ('groups', 'space')), parts along dimension 3, may hold values from -6 to 6
- forcing: bfloat16 [2, 4, 320, 8192], P('row', 'inst', None, ('groups', 'space')), parts along dimension 3, may hold values from -6 to 6
- metric_scale: float32 [2, 8192], P('row', ('groups', 'space')), parts along dimension 1, may hold values from 0.5 to 2
- frequency: float32 [1], replicated, may hold values from 0.1 to 0.4
- adjacency: int32 [2, 6, 8192], P('row', None, ('groups', 'space')), parts along dimension 2, may hold values from 0 to 1151, as said below
- partner: int32 [2, 4, 512], P('row', 'inst', ('groups', 'space')), parts along dimension 2, may hold values from 0 to 255, as said below
- volume_matrix: bfloat16 [320, 320], replicated, may hold values from -0.3125 to 0.3125
- trace_matrix: bfloat16 [480, 320], replicated, may hold values from -0.3125 to 0.3125
- lift_matrix: bfloat16 [320, 480], replicated, may hold values from -0.25 to 0.25
- block_inverse: bfloat16 [320, 320], replicated, may hold values from -0.3125 to 0.3125
Outputs:
- updated: bfloat16 [2, 4, 320, 8192], P('row', 'inst', None, ('groups', 'space')), parts along dimension 3
The draws below stay inside these ranges and needn't reach their ends.
There are 2 independent parts, one for each index of `groups`. The reference program is written for one: setup_inputs(seed, part) draws one part's arguments, and reference() takes and returns one part's arrays. A program takes and returns all parts, laid end to end along the dimension named above; an argument that names none is the same for every part. Nothing has to cross between parts.
Inputs may be any that keep to these rules, and one draw needn't show every extreme that they name: The element beside e across face f is (e - e % 1024 - 64 + adjacency[s, f, e]) mod 4096 of the same section, never e itself; the relation is mutual (the element beside e across f has e beside it across face f xor 1); faces 0 to 3 stay within e's block of 1024 elements, and faces 4 and 5 leave it only from the first or the last 64 elements of a block. partner[0, n] is a permutation of the 256 interface rows and partner[1, n] its inverse; for every instance, exactly 16 of the rows k with the same k // 64 map to each block of 64 rows.
All inputs are finite; a program needn't handle non-finite values.
Results may differ from the reference program's by a relative error of at most 0.0054.
Values may be sent and summed in bfloat16 or wider, within the bound.
A program may use at most 64 MiB of HBM per device.

```python
import math
import jax
import jax.numpy as jnp
from jax import lax

DOF = 320
TRACE = 80
LAYER = 64
E_DEV = 1024
RIM = 64
NF_DEV = 64
NI = 4
NE = 4096
NF = 256
CAP = 16


def draw_adjacency(key, part):
    side_cells = 8
    layers_all = NE // LAYER
    keys = jax.random.split(key, 2 * layers_all)
    orders = jax.vmap(lambda single: jax.random.permutation(single, LAYER))(keys).reshape(2, layers_all, LAYER).astype(jnp.int32)
    inverse = jnp.argsort(orders, axis=2).astype(jnp.int32)
    column = orders % side_cells
    line = orders // side_cells
    moves = [(0, line * side_cells + (column - 1) % side_cells), (0, line * side_cells + (column + 1) % side_cells), (0, (line - 1) % side_cells * side_cells + column), (0, (line + 1) % side_cells * side_cells + column), (-1, orders), (1, orders)]
    layer_ids = jnp.arange(layers_all, dtype=jnp.int32)[None, :, None]
    slot_ids = jnp.arange(LAYER, dtype=jnp.int32)[None, None, :]
    own_ids = layer_ids * LAYER + slot_ids
    own_start = own_ids // E_DEV * E_DEV
    faces_out = []
    for layer_step, target_pos in moves:
        rolled = jnp.roll(inverse, -layer_step, axis=1)
        target_slot = jnp.take_along_axis(rolled, target_pos, axis=2)
        target_layer = (layer_ids + layer_step) % layers_all
        target_ids = target_layer * LAYER + target_slot
        local_ids = jnp.mod(target_ids - own_start + RIM, NE)
        faces_out.append(local_ids.reshape(2, NE))
    return jnp.stack(faces_out, axis=1).astype(jnp.int32)


def draw_partner(key, part):
    shards = NF // NF_DEV
    key_first, key_second, key_shift = jax.random.split(key, 3)
    first_keys = jax.random.split(key_first, NI * shards)
    second_keys = jax.random.split(key_second, NI * shards)
    first_perm = jax.vmap(lambda single: jax.random.permutation(single, NF_DEV))(first_keys).reshape(NI, shards, NF_DEV).astype(jnp.int32)
    second_perm = jax.vmap(lambda single: jax.random.permutation(single, NF_DEV))(second_keys).reshape(NI, shards, NF_DEV).astype(jnp.int32)
    shifts = jax.random.randint(key_shift, (NI, 1, 1), 0, shards).astype(jnp.int32)
    source_block = jnp.arange(shards, dtype=jnp.int32)[None, :, None]
    group_ids = first_perm // CAP
    within = first_perm % CAP
    target_block = jnp.mod(source_block + group_ids + shifts, shards)
    target_slot = source_block * CAP + within
    inst_ids = jnp.arange(NI, dtype=jnp.int32)[:, None, None]
    flat_perm = second_perm.reshape(NI * shards, NF_DEV)
    picked = flat_perm[(inst_ids * shards + target_block).reshape(-1), target_slot.reshape(-1)]
    rotor_side = (target_block * NF_DEV + picked.reshape(NI, shards, NF_DEV)).reshape(NI, NF).astype(jnp.int32)
    stator_side = jnp.argsort(rotor_side, axis=1).astype(jnp.int32)
    return jnp.stack([rotor_side, stator_side])


def level_of(rng, dims, cuts, low, high):
    loudness = 1.0
    for axis_at, blocks in cuts:
        heights = jax.random.uniform(jax.random.fold_in(jax.random.fold_in(rng, 6), axis_at), (blocks,), jnp.float32, low / len(cuts), high / len(cuts))
        loudness = loudness * jnp.repeat(jnp.exp(heights), dims[axis_at] // blocks).reshape((-1,) + (1,) * (len(dims) - 1 - axis_at))
    return loudness


def bell_draw(key, shape, scale, bound, cuts=(), kind=jnp.bfloat16):
    drawn = jax.random.normal(key, shape, jnp.float32) * scale
    if len(cuts) > 0:
        drawn = level_of(key, shape, cuts, -0.22, 0.18) * drawn
    return jnp.clip(drawn, min=-bound, max=bound).astype(kind)


def setup_inputs(seed: int = 0, part: int = 0) -> dict:
    seeds = jax.random.split(jax.random.key(seed), 11)
    part_keys = jax.random.split(jax.random.fold_in(seeds[10], part), 11)
    solution = bell_draw(part_keys[0], (2, NI, DOF, NE), 1.0, 6.0, ((0, 2), (1, 2), (3, 4)))
    forcing = bell_draw(part_keys[1], (2, NI, DOF, NE), 1.0, 6.0, ((0, 2), (1, 2), (3, 4)))
    metric_scale = jnp.clip(jnp.exp(math.log(2.0) - 1.3862944 * jax.random.uniform(part_keys[2], (2, NE), jnp.float32) ** level_of(part_keys[2], (2, NE), ((0, 2), (1, 4)), -0.2, 0.2)), 0.5, 2.0)
    frequency = jnp.clip(jnp.exp(jax.random.uniform(seeds[3], (1,), jnp.float32, math.log(0.1), math.log(0.4))), 0.1, 0.4)
    adjacency = draw_adjacency(jax.random.fold_in(jax.random.fold_in(seeds[10], part), 71), part)
    partner = draw_partner(jax.random.fold_in(jax.random.fold_in(seeds[10], part), 71), part)
    volume_matrix = bell_draw(seeds[6], (DOF, DOF), DOF ** -0.5, 0.3125)
    trace_matrix = bell_draw(seeds[7], (6 * TRACE, DOF), DOF ** -0.5, 0.3125)
    lift_matrix = bell_draw(seeds[8], (DOF, 6 * TRACE), (6 * TRACE) ** -0.5, 0.25)
    block_inverse = bell_draw(seeds[9], (DOF, DOF), DOF ** -0.5, 0.3125)
    return dict(solution=solution, forcing=forcing, metric_scale=metric_scale, frequency=frequency, adjacency=adjacency, partner=partner, volume_matrix=volume_matrix, trace_matrix=trace_matrix, lift_matrix=lift_matrix, block_inverse=block_inverse)


OPPOSITE = (1, 0, 3, 2, 5, 4)


def spectral_table(instances, frequency):
    positions = jnp.arange(instances, dtype=jnp.int32)
    distance = (positions[:, None] - positions[None, :]).astype(jnp.float32)
    parity = 1.0 - 2.0 * jnp.mod(positions[:, None] + positions[None, :], 2).astype(jnp.float32)
    angles = jnp.pi * distance / instances
    sine_values = jnp.where(distance == 0.0, 1.0, jnp.sin(angles))
    cotangent = jnp.where(distance == 0.0, 0.0, jnp.cos(angles) / sine_values)
    return frequency * 0.5 * parity * cotangent


def reference(solution, forcing, metric_scale, frequency, adjacency, partner, volume_matrix, trace_matrix, lift_matrix, block_inverse):
    weights_all = spectral_table(NI, frequency[0])
    element_ids = jnp.arange(NE, dtype=jnp.int32)
    shard_start = (element_ids // E_DEV) * E_DEV
    neighbour_ids = jnp.mod(shard_start[None, None, :] - RIM + adjacency, NE).astype(jnp.int32)
    iface_ids = jnp.arange(NF, dtype=jnp.int32)
    iface_elems = ((iface_ids // NF_DEV) * E_DEV + iface_ids % NF_DEV).astype(jnp.int32)
    trace_wide = trace_matrix.astype(jnp.float32)
    lift_wide = lift_matrix.astype(jnp.float32)
    volume_wide = volume_matrix.astype(jnp.float32)
    inverse_wide = block_inverse.astype(jnp.float32)
    scales = metric_scale[:, None, :]

    def one_instance(number):
        current = solution[:, number]
        traces = jnp.einsum("fd,sde->sfe", trace_wide, current.astype(jnp.float32)).astype(jnp.bfloat16)
        gathered = []
        for side_number in range(2):
            pieces = []
            for face_number in range(6):
                facing = OPPOSITE[face_number]
                face_values = traces[side_number, facing * TRACE:(facing + 1) * TRACE]
                pieces.append(jnp.take(face_values, neighbour_ids[side_number, face_number], axis=1))
            beside = jnp.concatenate(pieces, axis=0)
            opposite_side = 1 - side_number
            partner_elems = jnp.take(iface_elems, partner[side_number, number], axis=0)
            incoming = jnp.take(traces[opposite_side, side_number * TRACE:(side_number + 1) * TRACE], partner_elems, axis=1)
            row_offset = opposite_side * TRACE
            beside = beside.at[row_offset:row_offset + TRACE, iface_elems].set(incoming)
            gathered.append(beside)
        beside_all = jnp.stack(gathered)
        coupled = jnp.einsum("df,sfe->sde", lift_wide, beside_all.astype(jnp.float32))
        volume = jnp.einsum("dk,ske->sde", volume_wide, current.astype(jnp.float32))
        source = jnp.einsum("m,smde->sde", weights_all[number], solution.astype(jnp.float32), precision=lax.Precision.HIGHEST).astype(jnp.bfloat16)
        residual = (forcing[:, number].astype(jnp.float32) - scales * (volume + coupled) - source.astype(jnp.float32)).astype(jnp.bfloat16)
        update = jnp.einsum("dk,ske->sde", inverse_wide, residual.astype(jnp.float32))
        return (current.astype(jnp.float32) + update / scales).astype(jnp.bfloat16)

    result = lax.map(one_instance, jnp.arange(NI, dtype=jnp.int32))
    return jnp.transpose(result, (1, 0, 2, 3))
```

```python
import functools

import jax
import jax.numpy as jnp
import numpy as np
from jax import lax
from jax.experimental import pallas as pl
from jax.experimental.pallas import tpu as pltpu
from jax.sharding import PartitionSpec as P

LAYER = 64
LANES = 128
CHUNK = 128
TILE = 256
OPPOSITE = (1, 0, 3, 2, 5, 4)
MESH = pl.DeviceIdType.MESH


def spectral_constants(instances):
    positions = np.arange(instances)
    distance = (positions[:, None] - positions[None, :]).astype(np.float32)
    parity = (1.0 - 2.0 * np.mod(positions[:, None] + positions[None, :], 2)).astype(np.float32)
    angles = (np.float32(np.pi) * distance / np.float32(instances)).astype(np.float32)
    sine_values = np.where(distance == 0.0, np.float32(1.0), np.sin(angles))
    cotangent = np.where(distance == 0.0, np.float32(0.0), np.cos(angles) / sine_values)
    return (np.float32(0.5) * parity * cotangent).astype(np.float32)


def one_hot(ids, first, rows):
    numbers = lax.broadcasted_iota(jnp.int32, (rows, ids.shape[1]), 0) + first
    return jnp.where(numbers == ids, 1.0, 0.0).astype(jnp.bfloat16)


def mm(a, b):
    return jnp.dot(a, b, preferred_element_type=jnp.float32)


def kernel(
    insts,
    shards,
    frequency,
    table_hbm,
    scales_hbm,
    adjacency_hbm,
    partner_hbm,
    solution_hbm,
    forcing_hbm,
    volume_hbm,
    trace_hbm,
    lift_hbm,
    inverse_hbm,
    result,
    table,
    scales,
    adjacency,
    partner,
    current,
    forcing,
    volume_matrix,
    trace_turned,
    trace_matrix,
    lift_matrix,
    inverse,
    others,
    traces,
    beside,
    partial,
    halos,
    crossed,
    load_sem,
    inst_send,
    inst_recv,
    halo_send,
    halo_recv,
    cross_send,
    cross_recv,
    above,
    ready,
    met,
    opened,
):
    local, dof, elements = current.shape
    width = trace_matrix.shape[0] // 6
    iface = partner.shape[2]
    parts = split(local, elements)
    my_inst = lax.axis_index("inst")
    my_space = lax.axis_index("space")
    section = lax.axis_index("row")
    right = lax.rem(my_space + 1, shards)
    left = lax.rem(my_space + shards - 1, shards)

    barrier = pltpu.get_barrier_semaphore()
    def signal(semaphore, target):
        pl.semaphore_signal(semaphore, inc=1, device_id=target, device_id_type=MESH)

    leads = my_inst == 0
    other_row = {"row": 1 - section}
    peers = [{"inst": lax.rem(my_inst + k, insts)} for k in range(1, insts)]
    for peer in peers:
        signal(barrier, peer)

    @pl.when(leads)
    def _():
        signal(barrier, other_row)

    @pl.when(jnp.logical_and(leads, my_space < shards - 1))
    def _():
        signal(barrier, {"space": my_space + 1})

    greeted = jnp.where(leads, 1 + jnp.minimum(my_space, 1), 0)
    pl.semaphore_wait(barrier, insts - 1 + greeted)

    def inst_copy(k, part):
        picked, start, stop = parts[part]
        return pltpu.make_async_remote_copy(
            src_ref=solution_hbm.at[0, picked, :, start:stop],
            dst_ref=others.at[k - 1, picked, :, start:stop],
            send_sem=inst_send.at[k - 1],
            recv_sem=inst_recv.at[k - 1, part],
            device_id={"inst": lax.rem(my_inst + k, insts)},
            device_id_type=MESH,
        )

    for part in range(len(parts)):
        for k in range(1, insts):
            inst_copy(k, part).start()

    loads = []
    for number, (source, target) in enumerate(
        (
            (trace_hbm, trace_turned),
            (solution_hbm.at[0], current),
            (volume_hbm, volume_matrix),
            (lift_hbm, lift_matrix),
            (forcing_hbm.at[0], forcing),
            (inverse_hbm, inverse),
            (adjacency_hbm, adjacency),
            (partner_hbm, partner),
            (scales_hbm, scales),
            (table_hbm, table),
        )
    ):
        copy = pltpu.make_async_copy(source, target, load_sem.at[min(number, 3)])
        copy.start()
        loads.append(copy)

    @pl.when(jnp.logical_and(leads, my_space == shards - 1))
    def _():
        signal(above, {"space": my_space - 1})

    loads[0].wait()
    trace_matrix[...] = trace_turned[...].T
    loads[1].wait()

    def trace_tile(t, carry):
        columns = pl.ds(pl.multiple_of(t * TILE, TILE), TILE)
        for n in range(local):
            values = mm(trace_matrix[...], current[n, :, columns]).astype(jnp.bfloat16)
            for f in range(6):
                traces[f, n * width : (n + 1) * width, columns] = values[
                    f * width : (f + 1) * width
                ]
        return carry

    lax.fori_loop(0, elements // TILE, trace_tile, 0)

    @pl.when(jnp.logical_and(leads, my_space < shards - 1))
    def _():
        pl.semaphore_wait(above, 1)

    @pl.when(jnp.logical_and(leads, jnp.logical_and(my_space > 0, my_space < shards - 1)))
    def _():
        signal(above, {"space": my_space - 1})

    @pl.when(jnp.logical_and(leads, my_space == 0))
    def _():
        for j in range(1, shards):
            signal(ready, {"space": j})

    loads[2].wait()

    def volume_tile(t, carry):
        columns = pl.ds(pl.multiple_of(t * TILE, TILE), TILE)
        for n in range(local):
            partial[n, :, columns] = mm(volume_matrix[...], current[n, :, columns])
        return carry

    lax.fori_loop(0, elements // TILE, volume_tile, 0)

    @pl.when(jnp.logical_and(leads, my_space > 0))
    def _():
        pl.semaphore_wait(ready, 1)

    @pl.when(leads)
    def _():
        signal(met, other_row)
        pl.semaphore_wait(met, 1)
        for peer in peers:
            signal(opened, peer)

    @pl.when(jnp.logical_not(leads))
    def _():
        pl.semaphore_wait(opened, 1)

    to_left = pltpu.make_async_remote_copy(
        src_ref=traces.at[4:6, :, 0:LANES],
        dst_ref=halos.at[1],
        send_sem=halo_send,
        recv_sem=halo_recv,
        device_id={"space": left},
        device_id_type=MESH,
    )
    to_right = pltpu.make_async_remote_copy(
        src_ref=traces.at[4:6, :, elements - LANES : elements],
        dst_ref=halos.at[0],
        send_sem=halo_send,
        recv_sem=halo_recv,
        device_id={"space": right},
        device_id_type=MESH,
    )
    to_left.start()
    to_right.start()

    def cross_copy(j, slot):
        return pltpu.make_async_remote_copy(
            src_ref=traces.at[1 - section, :, 0:LANES],
            dst_ref=crossed.at[slot],
            send_sem=cross_send,
            recv_sem=cross_recv,
            device_id={"space": j, "row": 1 - section},
            device_id_type=MESH,
        )

    for j in range(shards):
        cross_copy(j, my_space).start()

    def put(face, columns, values):
        for n in range(local):
            beside[n, face * width : (face + 1) * width, columns] = values[
                n * width : (n + 1) * width
            ].astype(jnp.bfloat16)

    for copy in loads[3:]:
        copy.wait()
    for face in range(6):

        def gather_tile(t, carry, face=face):
            columns = pl.ds(pl.multiple_of(t * TILE, TILE), TILE)
            ids = adjacency[face, :, columns]
            put(face, columns, mm(traces[OPPOSITE[face]], one_hot(ids, LAYER, elements)))
            return carry

        lax.fori_loop(0, elements // TILE, gather_tile, 0)

    both = pltpu.make_async_remote_copy(
        src_ref=halos,
        dst_ref=halos,
        send_sem=halo_send,
        recv_sem=halo_recv,
        device_id={"space": left},
        device_id_type=MESH,
    )
    both.wait()
    ends = (0,) if elements == LANES else (0, elements - LANES)
    for face in (4, 5):
        for start in ends:
            columns = pl.ds(start, LANES)
            ids = adjacency[face, :, columns]
            facing = OPPOSITE[face] - 4
            low = mm(halos[0, facing], one_hot(ids, LAYER - LANES, LANES))
            high = mm(halos[1, facing], one_hot(ids, LAYER + elements, LANES))
            for n in range(local):
                rows = slice(face * width, (face + 1) * width)
                lines = slice(n * width, (n + 1) * width)
                beside[n, rows, columns] = (
                    beside[n, rows, columns].astype(jnp.float32) + low[lines] + high[lines]
                ).astype(jnp.bfloat16)

    every = pltpu.make_async_remote_copy(
        src_ref=crossed,
        dst_ref=crossed,
        send_sem=cross_send,
        recv_sem=cross_recv,
        device_id={"row": 1 - section},
        device_id_type=MESH,
    )
    every.wait()
    for n in range(local):
        ids = partner[0, n : n + 1, :]
        lines = slice(n * width, (n + 1) * width)
        total = jnp.zeros((width, iface), jnp.float32)
        for j in range(shards):
            hot = one_hot(ids, j * iface, iface)
            total += mm(crossed[j, lines, 0:iface], hot)
        incoming = total.astype(jnp.bfloat16)
        for face in range(2):
            rows = slice(face * width, (face + 1) * width)
            beside[n, rows, 0:iface] = jnp.where(
                section == 1 - face, incoming, beside[n, rows, 0:iface]
            )

    factor = frequency[0]
    all_inst = local * insts

    def weight(n, owner, m):
        return factor * table[(my_inst * local + n) * all_inst + owner * local + m]

    def lift_tile(t, carry):
        columns = pl.ds(pl.multiple_of(t * TILE, TILE), TILE)
        scale = scales[:, columns]
        inverse_scale = 1.0 / scale
        for n in range(local):
            coupled = mm(lift_matrix[...], beside[n, :, columns])
            residual = forcing[n, :, columns].astype(jnp.float32) - scale * (
                partial[n, :, columns] + coupled
            )
            for m in range(local):
                residual -= weight(n, my_inst, m) * current[m, :, columns].astype(jnp.float32)
            update = mm(inverse[...], residual.astype(jnp.bfloat16))
            partial[n, :, columns] = (
                current[n, :, columns].astype(jnp.float32) + update * inverse_scale
            )
        return carry

    lax.fori_loop(0, elements // TILE, lift_tile, 0)

    for part, (picked, start, stop) in enumerate(parts):
        chosen = range(local)[picked]
        wide = min(TILE, stop - start)
        for k in range(1, insts):
            owner = lax.rem(my_inst + insts - k, insts)
            last = k == insts - 1 and chosen[-1] == local - 1
            inst_copy(k, part).wait_recv()

            def turn_tile(t, carry):
                columns = pl.ds(pl.multiple_of(start + t * wide, wide), wide)
                inverse_scale = 1.0 / scales[:, columns]
                values = [partial[n, :, columns] for n in range(local)]
                for m in chosen:
                    update = mm(inverse[...], others[k - 1, m, :, columns]) * inverse_scale
                    values = [values[n] - weight(n, owner, m) * update for n in range(local)]
                for n in range(local):
                    if last:
                        result[0, n, :, columns] = values[n].astype(jnp.bfloat16)
                    else:
                        partial[n, :, columns] = values[n]
                return carry

            lax.fori_loop(0, (stop - start) // wide, turn_tile, 0)

    if insts == 1:
        result[0] = partial[...].astype(jnp.bfloat16)

    for k in range(1, insts):
        pltpu.make_async_remote_copy(
            src_ref=solution_hbm.at[0],
            dst_ref=others.at[k - 1],
            send_sem=inst_send.at[k - 1],
            recv_sem=inst_recv.at[k - 1, 0],
            device_id={"inst": lax.rem(my_inst + k, insts)},
            device_id_type=MESH,
        ).wait_send()


def split(local, elements):
    parts = []
    start = 0
    while elements - start > CHUNK:
        stop = start + max(CHUNK, (elements - start) // (2 * CHUNK) * CHUNK)
        parts.append((slice(0, local), start, stop))
        start = stop
    return parts + [(slice(m, m + 1), start, elements) for m in range(local)]


def body(
    solution,
    forcing,
    metric_scale,
    frequency,
    adjacency,
    partner,
    volume_matrix,
    trace_matrix,
    lift_matrix,
    block_inverse,
):
    insts = lax.axis_size("inst")
    shards = lax.axis_size("space")
    _, local, dof, elements = solution.shape
    width = trace_matrix.shape[0] // 6
    parts = split(local, elements)
    table = jnp.asarray(spectral_constants(local * insts).reshape(-1))
    vmem = pl.BlockSpec(memory_space=pltpu.VMEM)
    away = pl.BlockSpec(memory_space=pltpu.HBM)
    narrow = jnp.bfloat16
    grant = 67043328 - 2 * solution.size - 65536
    dma = pltpu.SemaphoreType.DMA
    return pl.pallas_call(
        functools.partial(kernel, insts, shards),
        name="sweep",
        out_shape=pltpu.VMEM(solution.shape, narrow),
        in_specs=[pl.BlockSpec(memory_space=pltpu.SMEM)] + [away] * 10,
        out_specs=vmem,
        scratch_shapes=[
            pltpu.SMEM(table.shape, jnp.float32),
            pltpu.VMEM(metric_scale.shape, jnp.float32),
            pltpu.VMEM((6, 1, elements), jnp.int32),
            pltpu.VMEM(partner.shape, jnp.int32),
            pltpu.VMEM((local, dof, elements), narrow),
            pltpu.VMEM((local, dof, elements), narrow),
            pltpu.VMEM(volume_matrix.shape, narrow),
            pltpu.VMEM(trace_matrix.shape[::-1], narrow),
            pltpu.VMEM(trace_matrix.shape, narrow),
            pltpu.VMEM(lift_matrix.shape, narrow),
            pltpu.VMEM(block_inverse.shape, narrow),
            pltpu.VMEM((max(insts - 1, 1), local, dof, elements), narrow),
            pltpu.VMEM((6, local * width, elements), narrow),
            pltpu.VMEM((local, 6 * width, elements), narrow),
            pltpu.VMEM((local, dof, elements), jnp.float32),
            pltpu.VMEM((2, 2, local * width, LANES), narrow),
            pltpu.VMEM((shards, local * width, LANES), narrow),
            dma((4,)),
            dma((max(insts - 1, 1),)),
            dma((max(insts - 1, 1), len(parts))),
            dma,
            dma,
            dma,
            dma,
            pltpu.SemaphoreType.REGULAR,
            pltpu.SemaphoreType.REGULAR,
            pltpu.SemaphoreType.REGULAR,
            pltpu.SemaphoreType.REGULAR,
        ],
        compiler_params=pltpu.CompilerParams(
            collective_id=0, has_side_effects=True, vmem_limit_bytes=grant
        ),
    )(
        frequency,
        table,
        metric_scale,
        jnp.transpose(adjacency, (1, 0, 2)),
        partner,
        solution,
        forcing,
        volume_matrix,
        trace_matrix.T,
        lift_matrix,
        block_inverse,
    )


def solution(mesh):
    in_specs = (
        P("row", "inst", None, ("groups", "space")),
        P("row", "inst", None, ("groups", "space")),
        P("row", ("groups", "space")),
        P(),
        P("row", None, ("groups", "space")),
        P("row", "inst", ("groups", "space")),
        P(),
        P(),
        P(),
        P(),
    )
    out_specs = P("row", "inst", None, ("groups", "space"))
    return jax.shard_map(body, mesh=mesh, in_specs=in_specs, out_specs=out_specs, check_vma=False)
```

```python
import functools

import jax
import jax.numpy as jnp
import numpy as np
from jax import lax
from jax.experimental import pallas as pl
from jax.experimental.pallas import tpu as pltpu
from jax.sharding import PartitionSpec as P

LAYER = 64
LANES = 128
CHUNK = 128
TILE = 256
OPPOSITE = (1, 0, 3, 2, 5, 4)
MESH = pl.DeviceIdType.MESH


def spectral_constants(instances):
    positions = np.arange(instances)
    distance = (positions[:, None] - positions[None, :]).astype(np.float32)
    parity = (1.0 - 2.0 * np.mod(positions[:, None] + positions[None, :], 2)).astype(np.float32)
    angles = (np.float32(np.pi) * distance / np.float32(instances)).astype(np.float32)
    sine_values = np.where(distance == 0.0, np.float32(1.0), np.sin(angles))
    cotangent = np.where(distance == 0.0, np.float32(0.0), np.cos(angles) / sine_values)
    return (np.float32(0.5) * parity * cotangent).astype(np.float32)


def one_hot(ids, first, rows):
    numbers = lax.broadcasted_iota(jnp.int32, (rows, ids.shape[1]), 0) + first
    return jnp.where(numbers == ids, 1.0, 0.0).astype(jnp.bfloat16)


def mm(a, b):
    return jnp.dot(a, b, preferred_element_type=jnp.float32)


def kernel(
    insts,
    shards,
    frequency,
    table_hbm,
    scales_hbm,
    adjacency_hbm,
    partner_hbm,
    solution_hbm,
    forcing_hbm,
    volume_hbm,
    trace_hbm,
    lift_hbm,
    inverse_hbm,
    result,
    table,
    scales,
    adjacency,
    partner,
    current,
    forcing,
    volume_matrix,
    trace_turned,
    trace_matrix,
    lift_matrix,
    inverse,
    others,
    traces,
    beside,
    partial,
    halos,
    crossed,
    load_sem,
    inst_send,
    inst_recv,
    halo_send,
    halo_recv,
    cross_send,
    cross_recv,
    above,
    ready,
    met,
    opened,
    relayed,
    relay_send,
    relay_recv,
    onward_send,
):
    local, dof, elements = current.shape
    width = trace_matrix.shape[0] // 6
    iface = partner.shape[2]
    parts = split(local, elements)
    my_inst = lax.axis_index("inst")
    my_space = lax.axis_index("space")
    section = lax.axis_index("row")
    right = lax.rem(my_space + 1, shards)
    left = lax.rem(my_space + shards - 1, shards)

    barrier = pltpu.get_barrier_semaphore()
    def signal(semaphore, target):
        pl.semaphore_signal(semaphore, inc=1, device_id=target, device_id_type=MESH)

    leads = my_inst == 0
    other_row = {"row": 1 - section}
    peers = [{"inst": lax.rem(my_inst + k, insts)} for k in range(1, insts)]
    for peer in peers:
        signal(barrier, peer)

    @pl.when(leads)
    def _():
        signal(barrier, other_row)

    @pl.when(jnp.logical_and(leads, my_space < shards - 1))
    def _():
        signal(barrier, {"space": my_space + 1})

    greeted = jnp.where(leads, 1 + jnp.minimum(my_space, 1), 0)
    pl.semaphore_wait(barrier, insts - 1 + greeted)

    def inst_copy(k, part):
        picked, start, stop = parts[part]
        return pltpu.make_async_remote_copy(
            src_ref=solution_hbm.at[0, picked, :, start:stop],
            dst_ref=others.at[k - 1, picked, :, start:stop],
            send_sem=inst_send.at[k - 1],
            recv_sem=inst_recv.at[k - 1, part],
            device_id={"inst": lax.rem(my_inst + k, insts)},
            device_id_type=MESH,
        )

    early = range(1, 2 + min(local - 1, 1))
    late = range(early.stop, len(parts))

    def send(numbers):
        for part in numbers:
            for k in range(1, insts):
                inst_copy(k, part).start()

    @pl.when(section == 0)
    def _():
        send(early)
        send(late)

    @pl.when(section == 1)
    def _():
        send(range(early.stop))

    relay = pltpu.make_async_remote_copy(
        src_ref=solution_hbm.at[0, 0, :, 0:CHUNK],
        dst_ref=relayed,
        send_sem=relay_send,
        recv_sem=relay_recv,
        device_id=other_row,
        device_id_type=MESH,
    )

    def onward(k):
        return pltpu.make_async_remote_copy(
            src_ref=relayed,
            dst_ref=others.at[k - 1, 0, :, 0:CHUNK],
            send_sem=onward_send,
            recv_sem=inst_recv.at[k - 1, 0],
            device_id={"inst": lax.rem(my_inst + k, insts), "row": 0},
            device_id_type=MESH,
        )

    loads = []
    for number, (source, target) in enumerate(
        (
            (trace_hbm, trace_turned),
            (solution_hbm.at[0], current),
            (volume_hbm, volume_matrix),
            (lift_hbm, lift_matrix),
            (forcing_hbm.at[0], forcing),
            (inverse_hbm, inverse),
            (adjacency_hbm, adjacency),
            (partner_hbm, partner),
            (scales_hbm, scales),
            (table_hbm, table),
        )
    ):
        copy = pltpu.make_async_copy(source, target, load_sem.at[min(number, 3)])
        copy.start()
        loads.append(copy)

    @pl.when(jnp.logical_and(leads, my_space == shards - 1))
    def _():
        signal(above, {"space": my_space - 1})

    loads[0].wait()
    trace_matrix[...] = trace_turned[...].T
    loads[1].wait()

    def trace_tile(t, carry):
        columns = pl.ds(pl.multiple_of(t * TILE, TILE), TILE)
        for n in range(local):
            values = mm(trace_matrix[...], current[n, :, columns]).astype(jnp.bfloat16)
            for f in range(6):
                traces[f, n * width : (n + 1) * width, columns] = values[
                    f * width : (f + 1) * width
                ]
        return carry

    lax.fori_loop(0, elements // TILE, trace_tile, 0)

    @pl.when(jnp.logical_and(leads, my_space < shards - 1))
    def _():
        pl.semaphore_wait(above, 1)

    @pl.when(jnp.logical_and(leads, jnp.logical_and(my_space > 0, my_space < shards - 1)))
    def _():
        signal(above, {"space": my_space - 1})

    @pl.when(jnp.logical_and(leads, my_space == 0))
    def _():
        for j in range(1, shards):
            signal(ready, {"space": j})

    loads[2].wait()

    def volume_tile(t, carry):
        columns = pl.ds(pl.multiple_of(t * TILE, TILE), TILE)
        for n in range(local):
            partial[n, :, columns] = mm(volume_matrix[...], current[n, :, columns])
        return carry

    lax.fori_loop(0, elements // TILE, volume_tile, 0)

    @pl.when(jnp.logical_and(leads, my_space > 0))
    def _():
        pl.semaphore_wait(ready, 1)

    @pl.when(leads)
    def _():
        signal(met, other_row)
        pl.semaphore_wait(met, 1)
        for peer in peers:
            signal(opened, peer)

    @pl.when(jnp.logical_not(leads))
    def _():
        pl.semaphore_wait(opened, 1)

    @pl.when(section == 0)
    def _():
        relay.start()

    to_left = pltpu.make_async_remote_copy(
        src_ref=traces.at[4:6, :, 0:LANES],
        dst_ref=halos.at[1],
        send_sem=halo_send,
        recv_sem=halo_recv,
        device_id={"space": left},
        device_id_type=MESH,
    )
    to_right = pltpu.make_async_remote_copy(
        src_ref=traces.at[4:6, :, elements - LANES : elements],
        dst_ref=halos.at[0],
        send_sem=halo_send,
        recv_sem=halo_recv,
        device_id={"space": right},
        device_id_type=MESH,
    )
    to_left.start()
    to_right.start()

    def cross_copy(j, slot):
        return pltpu.make_async_remote_copy(
            src_ref=traces.at[1 - section, :, 0:LANES],
            dst_ref=crossed.at[slot],
            send_sem=cross_send,
            recv_sem=cross_recv,
            device_id={"space": j, "row": 1 - section},
            device_id_type=MESH,
        )

    for j in range(shards):
        cross_copy(j, my_space).start()

    def put(face, columns, values):
        for n in range(local):
            beside[n, face * width : (face + 1) * width, columns] = values[
                n * width : (n + 1) * width
            ].astype(jnp.bfloat16)

    for copy in loads[3:]:
        copy.wait()
    for face in range(6):

        def gather_tile(t, carry, face=face):
            columns = pl.ds(pl.multiple_of(t * TILE, TILE), TILE)
            ids = adjacency[face, :, columns]
            put(face, columns, mm(traces[OPPOSITE[face]], one_hot(ids, LAYER, elements)))
            return carry

        lax.fori_loop(0, elements // TILE, gather_tile, 0)
        if face == 1:

            @pl.when(section == 1)
            def _():
                relay.wait_recv()
                for k in range(1, insts):
                    onward(k).start()
                send(late)

    both = pltpu.make_async_remote_copy(
        src_ref=halos,
        dst_ref=halos,
        send_sem=halo_send,
        recv_sem=halo_recv,
        device_id={"space": left},
        device_id_type=MESH,
    )
    both.wait()
    ends = (0,) if elements == LANES else (0, elements - LANES)
    for face in (4, 5):
        for start in ends:
            columns = pl.ds(start, LANES)
            ids = adjacency[face, :, columns]
            facing = OPPOSITE[face] - 4
            low = mm(halos[0, facing], one_hot(ids, LAYER - LANES, LANES))
            high = mm(halos[1, facing], one_hot(ids, LAYER + elements, LANES))
            for n in range(local):
                rows = slice(face * width, (face + 1) * width)
                lines = slice(n * width, (n + 1) * width)
                beside[n, rows, columns] = (
                    beside[n, rows, columns].astype(jnp.float32) + low[lines] + high[lines]
                ).astype(jnp.bfloat16)

    every = pltpu.make_async_remote_copy(
        src_ref=crossed,
        dst_ref=crossed,
        send_sem=cross_send,
        recv_sem=cross_recv,
        device_id={"row": 1 - section},
        device_id_type=MESH,
    )
    every.wait()
    for n in range(local):
        ids = partner[0, n : n + 1, :]
        lines = slice(n * width, (n + 1) * width)
        total = jnp.zeros((width, iface), jnp.float32)
        for j in range(shards):
            hot = one_hot(ids, j * iface, iface)
            total += mm(crossed[j, lines, 0:iface], hot)
        incoming = total.astype(jnp.bfloat16)
        for face in range(2):
            rows = slice(face * width, (face + 1) * width)
            beside[n, rows, 0:iface] = jnp.where(
                section == 1 - face, incoming, beside[n, rows, 0:iface]
            )

    factor = frequency[0]
    all_inst = local * insts

    def weight(n, owner, m):
        return factor * table[(my_inst * local + n) * all_inst + owner * local + m]

    def lift_tile(t, carry):
        columns = pl.ds(pl.multiple_of(t * TILE, TILE), TILE)
        scale = scales[:, columns]
        inverse_scale = 1.0 / scale
        for n in range(local):
            coupled = mm(lift_matrix[...], beside[n, :, columns])
            residual = forcing[n, :, columns].astype(jnp.float32) - scale * (
                partial[n, :, columns] + coupled
            )
            for m in range(local):
                residual -= weight(n, my_inst, m) * current[m, :, columns].astype(jnp.float32)
            update = mm(inverse[...], residual.astype(jnp.bfloat16))
            partial[n, :, columns] = (
                current[n, :, columns].astype(jnp.float32) + update * inverse_scale
            )
        return carry

    lax.fori_loop(0, elements // TILE, lift_tile, 0)

    for part, (picked, start, stop) in enumerate(parts):
        chosen = range(local)[picked]
        wide = TILE if (stop - start) % TILE == 0 else CHUNK
        for k in range(1, insts):
            owner = lax.rem(my_inst + insts - k, insts)
            last = k == insts - 1 and chosen[-1] == local - 1
            inst_copy(k, part).wait_recv()

            def turn_tile(t, carry):
                columns = pl.ds(pl.multiple_of(start + t * wide, wide), wide)
                inverse_scale = 1.0 / scales[:, columns]
                values = [partial[n, :, columns] for n in range(local)]
                for m in chosen:
                    update = mm(inverse[...], others[k - 1, m, :, columns]) * inverse_scale
                    values = [values[n] - weight(n, owner, m) * update for n in range(local)]
                for n in range(local):
                    if last:
                        result[0, n, :, columns] = values[n].astype(jnp.bfloat16)
                    else:
                        partial[n, :, columns] = values[n]
                return carry

            lax.fori_loop(0, (stop - start) // wide, turn_tile, 0)

    if insts == 1:
        result[0] = partial[...].astype(jnp.bfloat16)

    def sent(source, semaphore):
        pltpu.make_async_remote_copy(
            src_ref=source,
            dst_ref=source,
            send_sem=semaphore,
            recv_sem=relay_recv,
            device_id=other_row,
            device_id_type=MESH,
        ).wait_send()

    @pl.when(section == 0)
    def _():
        sent(relayed, relay_send)
        for k in range(1, insts):
            sent(others.at[k - 1, 0, :, CHUNK:], inst_send.at[k - 1])
            if local > 1:
                sent(others.at[k - 1, 1:], inst_send.at[k - 1])

    @pl.when(section == 1)
    def _():
        sent(others.at[:, 0, :, 0:CHUNK], onward_send)
        for k in range(1, insts):
            sent(others.at[k - 1], inst_send.at[k - 1])


def split(local, elements):
    half = elements // (2 * CHUNK) * CHUNK
    parts = [(slice(0, 1), 0, CHUNK), (slice(0, 1), CHUNK, half)]
    if local > 1:
        parts.append((slice(1, local), 0, half))
    start = half
    while elements - start > CHUNK:
        stop = start + max(CHUNK, (elements - start) // (2 * CHUNK) * CHUNK)
        parts.append((slice(0, local), start, stop))
        start = stop
    return parts + [(slice(m, m + 1), start, elements) for m in range(local)]


def body(
    solution,
    forcing,
    metric_scale,
    frequency,
    adjacency,
    partner,
    volume_matrix,
    trace_matrix,
    lift_matrix,
    block_inverse,
):
    insts = lax.axis_size("inst")
    shards = lax.axis_size("space")
    _, local, dof, elements = solution.shape
    width = trace_matrix.shape[0] // 6
    parts = split(local, elements)
    table = jnp.asarray(spectral_constants(local * insts).reshape(-1))
    vmem = pl.BlockSpec(memory_space=pltpu.VMEM)
    away = pl.BlockSpec(memory_space=pltpu.HBM)
    narrow = jnp.bfloat16
    grant = 67043328 - 2 * solution.size - 65536
    dma = pltpu.SemaphoreType.DMA
    return pl.pallas_call(
        functools.partial(kernel, insts, shards),
        name="sweep",
        out_shape=pltpu.VMEM(solution.shape, narrow),
        in_specs=[pl.BlockSpec(memory_space=pltpu.SMEM)] + [away] * 10,
        out_specs=vmem,
        scratch_shapes=[
            pltpu.SMEM(table.shape, jnp.float32),
            pltpu.VMEM(metric_scale.shape, jnp.float32),
            pltpu.VMEM((6, 1, elements), jnp.int32),
            pltpu.VMEM(partner.shape, jnp.int32),
            pltpu.VMEM((local, dof, elements), narrow),
            pltpu.VMEM((local, dof, elements), narrow),
            pltpu.VMEM(volume_matrix.shape, narrow),
            pltpu.VMEM(trace_matrix.shape[::-1], narrow),
            pltpu.VMEM(trace_matrix.shape, narrow),
            pltpu.VMEM(lift_matrix.shape, narrow),
            pltpu.VMEM(block_inverse.shape, narrow),
            pltpu.VMEM((max(insts - 1, 1), local, dof, elements), narrow),
            pltpu.VMEM((6, local * width, elements), narrow),
            pltpu.VMEM((local, 6 * width, elements), narrow),
            pltpu.VMEM((local, dof, elements), jnp.float32),
            pltpu.VMEM((2, 2, local * width, LANES), narrow),
            pltpu.VMEM((shards, local * width, LANES), narrow),
            dma((4,)),
            dma((max(insts - 1, 1),)),
            dma((max(insts - 1, 1), len(parts))),
            dma,
            dma,
            dma,
            dma,
            pltpu.SemaphoreType.REGULAR,
            pltpu.SemaphoreType.REGULAR,
            pltpu.SemaphoreType.REGULAR,
            pltpu.SemaphoreType.REGULAR,
            pltpu.VMEM((dof, CHUNK), narrow),
            dma,
            dma,
            dma,
        ],
        compiler_params=pltpu.CompilerParams(
            collective_id=0, has_side_effects=True, vmem_limit_bytes=grant
        ),
    )(
        frequency,
        table,
        metric_scale,
        jnp.transpose(adjacency, (1, 0, 2)),
        partner,
        solution,
        forcing,
        volume_matrix,
        trace_matrix.T,
        lift_matrix,
        block_inverse,
    )


def solution(mesh):
    in_specs = (
        P("row", "inst", None, ("groups", "space")),
        P("row", "inst", None, ("groups", "space")),
        P("row", ("groups", "space")),
        P(),
        P("row", None, ("groups", "space")),
        P("row", "inst", ("groups", "space")),
        P(),
        P(),
        P(),
        P(),
    )
    out_specs = P("row", "inst", None, ("groups", "space"))
    return jax.shard_map(body, mesh=mesh, in_specs=in_specs, out_specs=out_specs, check_vma=False)
```

```python
import functools

import jax
import jax.numpy as jnp
import numpy as np
from jax import lax
from jax.experimental import pallas as pl
from jax.experimental.pallas import tpu as pltpu
from jax.sharding import PartitionSpec as P

LAYER = 64
LANES = 128
CHUNK = 128
TILE = 256
OPPOSITE = (1, 0, 3, 2, 5, 4)
MESH = pl.DeviceIdType.MESH


def spectral_constants(instances):
    positions = np.arange(instances)
    distance = (positions[:, None] - positions[None, :]).astype(np.float32)
    parity = (1.0 - 2.0 * np.mod(positions[:, None] + positions[None, :], 2)).astype(np.float32)
    angles = (np.float32(np.pi) * distance / np.float32(instances)).astype(np.float32)
    sine_values = np.where(distance == 0.0, np.float32(1.0), np.sin(angles))
    cotangent = np.where(distance == 0.0, np.float32(0.0), np.cos(angles) / sine_values)
    return (np.float32(0.5) * parity * cotangent).astype(np.float32)


def one_hot(ids, first, rows):
    numbers = lax.broadcasted_iota(jnp.int32, (rows, ids.shape[1]), 0) + first
    return jnp.where(numbers == ids, 1.0, 0.0).astype(jnp.bfloat16)


def mm(a, b):
    return jnp.dot(a, b, preferred_element_type=jnp.float32)


def kernel(
    insts,
    shards,
    given,
    table_hbm,
    scales_hbm,
    adjacency_hbm,
    partner_hbm,
    solution_hbm,
    forcing_hbm,
    volume_hbm,
    trace_hbm,
    lift_hbm,
    inverse_hbm,
    result,
    table,
    scales,
    adjacency,
    partner,
    current,
    forcing,
    volume_matrix,
    trace_turned,
    trace_matrix,
    lift_matrix,
    inverse,
    others,
    traces,
    beside,
    partial,
    halos,
    crossed,
    load_sem,
    sending,
    inst_recv,
    halo_recv,
    cross_recv,
    above,
    ready,
    met,
    opened,
    relayed,
    relay_recv,
    frequency,
    frequency_recv,
):
    local, dof, elements = current.shape
    width = trace_matrix.shape[0] // 6
    iface = partner.shape[2]
    parts = split(local, elements)
    my_inst = lax.axis_index("inst")
    my_space = lax.axis_index("space")
    section = lax.axis_index("row")
    right = lax.rem(my_space + 1, shards)
    left = lax.rem(my_space + shards - 1, shards)

    barrier = pltpu.get_barrier_semaphore()
    def signal(semaphore, target):
        pl.semaphore_signal(semaphore, inc=1, device_id=target, device_id_type=MESH)

    leads = my_inst == 0
    other_row = {"row": 1 - section}
    peers = [{"inst": lax.rem(my_inst + k, insts)} for k in range(1, insts)]
    for peer in peers:
        signal(barrier, peer)

    @pl.when(leads)
    def _():
        signal(barrier, other_row)

    @pl.when(jnp.logical_and(leads, my_space < shards - 1))
    def _():
        signal(barrier, {"space": my_space + 1})

    greeted = jnp.where(leads, 1 + jnp.minimum(my_space, 1), 0)
    pl.semaphore_wait(barrier, insts - 1 + greeted)

    def inst_copy(k, part):
        picked, start, stop = parts[part]
        return pltpu.make_async_remote_copy(
            src_ref=solution_hbm.at[0, picked, :, start:stop],
            dst_ref=others.at[k - 1, picked, :, start:stop],
            send_sem=sending,
            recv_sem=inst_recv.at[k - 1, part],
            device_id={"inst": lax.rem(my_inst + k, insts)},
            device_id_type=MESH,
        )

    early = range(1, 2 + min(local - 1, 1))
    late = range(early.stop, len(parts))

    def send(numbers):
        for part in numbers:
            for k in range(1, insts):
                inst_copy(k, part).start()

    def share(k):
        return pltpu.make_async_remote_copy(
            src_ref=given,
            dst_ref=frequency,
            send_sem=sending,
            recv_sem=frequency_recv,
            device_id=peers[k - 1],
            device_id_type=MESH,
        )

    @pl.when(leads)
    def _():
        for k in range(1, insts):
            share(k).start()

    @pl.when(section == 0)
    def _():
        send(early)
        send(late)

    @pl.when(section == 1)
    def _():
        send(range(early.stop))

    relay = pltpu.make_async_remote_copy(
        src_ref=solution_hbm.at[0, 0, :, 0:CHUNK],
        dst_ref=relayed,
        send_sem=sending,
        recv_sem=relay_recv,
        device_id=other_row,
        device_id_type=MESH,
    )

    def onward(k):
        return pltpu.make_async_remote_copy(
            src_ref=relayed,
            dst_ref=others.at[k - 1, 0, :, 0:CHUNK],
            send_sem=sending,
            recv_sem=inst_recv.at[k - 1, 0],
            device_id={"inst": lax.rem(my_inst + k, insts), "row": 0},
            device_id_type=MESH,
        )

    loads = []
    for number, (source, target) in enumerate(
        (
            (trace_hbm, trace_turned),
            (solution_hbm.at[0], current),
            (volume_hbm, volume_matrix),
            (lift_hbm, lift_matrix),
            (forcing_hbm.at[0], forcing),
            (inverse_hbm, inverse),
            (adjacency_hbm, adjacency),
            (partner_hbm, partner),
            (scales_hbm, scales),
            (table_hbm, table),
        )
    ):
        copy = pltpu.make_async_copy(source, target, load_sem.at[min(number // 3, 1)])
        copy.start()
        loads.append(copy)

    @pl.when(jnp.logical_and(leads, my_space == shards - 1))
    def _():
        signal(above, {"space": my_space - 1})

    for copy in loads[:3]:
        copy.wait()
    trace_matrix[...] = trace_turned[...].T

    def trace_tile(t, carry):
        columns = pl.ds(pl.multiple_of(t * TILE, TILE), TILE)
        for n in range(local):
            values = mm(trace_matrix[...], current[n, :, columns]).astype(jnp.bfloat16)
            for f in range(6):
                traces[f, n * width : (n + 1) * width, columns] = values[
                    f * width : (f + 1) * width
                ]
        return carry

    lax.fori_loop(0, elements // TILE, trace_tile, 0)

    @pl.when(jnp.logical_and(leads, my_space < shards - 1))
    def _():
        pl.semaphore_wait(above, 1)

    @pl.when(jnp.logical_and(leads, jnp.logical_and(my_space > 0, my_space < shards - 1)))
    def _():
        signal(above, {"space": my_space - 1})

    @pl.when(jnp.logical_and(leads, my_space == 0))
    def _():
        for j in range(1, shards):
            signal(ready, {"space": j})

    def volume_tile(t, carry):
        columns = pl.ds(pl.multiple_of(t * TILE, TILE), TILE)
        for n in range(local):
            partial[n, :, columns] = mm(volume_matrix[...], current[n, :, columns])
        return carry

    lax.fori_loop(0, elements // TILE, volume_tile, 0)

    @pl.when(jnp.logical_and(leads, my_space > 0))
    def _():
        pl.semaphore_wait(ready, 1)

    @pl.when(leads)
    def _():
        signal(met, other_row)
        pl.semaphore_wait(met, 1)
        for peer in peers:
            signal(opened, peer)

    @pl.when(jnp.logical_not(leads))
    def _():
        pl.semaphore_wait(opened, 1)

    @pl.when(section == 0)
    def _():
        relay.start()

    to_left = pltpu.make_async_remote_copy(
        src_ref=traces.at[4:6, :, 0:LANES],
        dst_ref=halos.at[1],
        send_sem=sending,
        recv_sem=halo_recv,
        device_id={"space": left},
        device_id_type=MESH,
    )
    to_right = pltpu.make_async_remote_copy(
        src_ref=traces.at[4:6, :, elements - LANES : elements],
        dst_ref=halos.at[0],
        send_sem=sending,
        recv_sem=halo_recv,
        device_id={"space": right},
        device_id_type=MESH,
    )
    to_left.start()
    to_right.start()

    def cross_copy(j, slot):
        return pltpu.make_async_remote_copy(
            src_ref=traces.at[1 - section, :, 0:LANES],
            dst_ref=crossed.at[slot],
            send_sem=sending,
            recv_sem=cross_recv,
            device_id={"space": j, "row": 1 - section},
            device_id_type=MESH,
        )

    for j in range(shards):
        cross_copy(j, my_space).start()

    def put(face, columns, values):
        for n in range(local):
            beside[n, face * width : (face + 1) * width, columns] = values[
                n * width : (n + 1) * width
            ].astype(jnp.bfloat16)

    for copy in loads[3:]:
        copy.wait()
    for face in range(6):

        def gather_tile(t, carry, face=face):
            columns = pl.ds(pl.multiple_of(t * TILE, TILE), TILE)
            ids = adjacency[face, :, columns]
            put(face, columns, mm(traces[OPPOSITE[face]], one_hot(ids, LAYER, elements)))
            return carry

        lax.fori_loop(0, elements // TILE, gather_tile, 0)
        if face == 1:

            @pl.when(section == 1)
            def _():
                relay.wait_recv()
                for k in range(1, insts):
                    onward(k).start()
                send(late)

    both = pltpu.make_async_remote_copy(
        src_ref=halos,
        dst_ref=halos,
        send_sem=sending,
        recv_sem=halo_recv,
        device_id={"space": left},
        device_id_type=MESH,
    )
    both.wait_recv()
    ends = (0,) if elements == LANES else (0, elements - LANES)
    for face in (4, 5):
        for start in ends:
            columns = pl.ds(start, LANES)
            ids = adjacency[face, :, columns]
            facing = OPPOSITE[face] - 4
            low = mm(halos[0, facing], one_hot(ids, LAYER - LANES, LANES))
            high = mm(halos[1, facing], one_hot(ids, LAYER + elements, LANES))
            for n in range(local):
                rows = slice(face * width, (face + 1) * width)
                lines = slice(n * width, (n + 1) * width)
                beside[n, rows, columns] = (
                    beside[n, rows, columns].astype(jnp.float32) + low[lines] + high[lines]
                ).astype(jnp.bfloat16)

    every = pltpu.make_async_remote_copy(
        src_ref=crossed,
        dst_ref=crossed,
        send_sem=sending,
        recv_sem=cross_recv,
        device_id={"row": 1 - section},
        device_id_type=MESH,
    )
    every.wait_recv()
    for n in range(local):
        ids = partner[0, n : n + 1, :]
        lines = slice(n * width, (n + 1) * width)
        total = jnp.zeros((width, iface), jnp.float32)
        for j in range(shards):
            hot = one_hot(ids, j * iface, iface)
            total += mm(crossed[j, lines, 0:iface], hot)
        incoming = total.astype(jnp.bfloat16)
        for face in range(2):
            rows = slice(face * width, (face + 1) * width)
            beside[n, rows, 0:iface] = jnp.where(
                section == 1 - face, incoming, beside[n, rows, 0:iface]
            )


    @pl.when(leads)
    def _():
        frequency[...] = given[...]

    if insts > 1:

        @pl.when(jnp.logical_not(leads))
        def _():
            share(1).wait_recv()

    factor = frequency[0:1, 0:1]
    all_inst = local * insts

    def weight(n, owner, m):
        return factor * table[(my_inst * local + n) * all_inst + owner * local + m]

    def lift_tile(t, carry):
        columns = pl.ds(pl.multiple_of(t * TILE, TILE), TILE)
        scale = scales[:, columns]
        inverse_scale = 1.0 / scale
        for n in range(local):
            coupled = mm(lift_matrix[...], beside[n, :, columns])
            residual = forcing[n, :, columns].astype(jnp.float32) - scale * (
                partial[n, :, columns] + coupled
            )
            for m in range(local):
                residual -= weight(n, my_inst, m) * current[m, :, columns].astype(jnp.float32)
            update = mm(inverse[...], residual.astype(jnp.bfloat16))
            partial[n, :, columns] = (
                current[n, :, columns].astype(jnp.float32) + update * inverse_scale
            )
        return carry

    lax.fori_loop(0, elements // TILE, lift_tile, 0)

    for part, (picked, start, stop) in enumerate(parts):
        chosen = range(local)[picked]
        wide = TILE if (stop - start) % TILE == 0 else CHUNK
        for k in range(1, insts):
            owner = lax.rem(my_inst + insts - k, insts)
            last = k == insts - 1 and chosen[-1] == local - 1
            inst_copy(k, part).wait_recv()

            def turn_tile(t, carry):
                columns = pl.ds(pl.multiple_of(start + t * wide, wide), wide)
                inverse_scale = 1.0 / scales[:, columns]
                values = [partial[n, :, columns] for n in range(local)]
                for m in chosen:
                    update = mm(inverse[...], others[k - 1, m, :, columns]) * inverse_scale
                    values = [values[n] - weight(n, owner, m) * update for n in range(local)]
                for n in range(local):
                    if last:
                        result[0, n, :, columns] = values[n].astype(jnp.bfloat16)
                    else:
                        partial[n, :, columns] = values[n]
                return carry

            lax.fori_loop(0, (stop - start) // wide, turn_tile, 0)

    if insts == 1:
        result[0] = partial[...].astype(jnp.bfloat16)

    both.wait_send()
    every.wait_send()

    def sent(source):
        pltpu.make_async_remote_copy(
            src_ref=source,
            dst_ref=source,
            send_sem=sending,
            recv_sem=relay_recv,
            device_id=other_row,
            device_id_type=MESH,
        ).wait_send()

    @pl.when(leads)
    def _():
        for _ in peers:
            sent(frequency)

    @pl.when(section == 0)
    def _():
        sent(relayed)
        sent(others.at[:, 0, :, CHUNK:])
        if local > 1:
            sent(others.at[:, 1:])

    @pl.when(section == 1)
    def _():
        sent(others.at[:, 0, :, 0:CHUNK])
        sent(others)


def split(local, elements):
    half = elements // (2 * CHUNK) * CHUNK
    parts = [(slice(0, 1), 0, CHUNK), (slice(0, 1), CHUNK, half)]
    if local > 1:
        parts.append((slice(1, local), 0, half))
    start = half
    while elements - start > CHUNK:
        stop = start + max(CHUNK, (elements - start) // (2 * CHUNK) * CHUNK)
        parts.append((slice(0, local), start, stop))
        start = stop
    return parts + [(slice(m, m + 1), start, elements) for m in range(local)]


def body(
    solution,
    forcing,
    metric_scale,
    frequency,
    adjacency,
    partner,
    volume_matrix,
    trace_matrix,
    lift_matrix,
    block_inverse,
):
    insts = lax.axis_size("inst")
    shards = lax.axis_size("space")
    _, local, dof, elements = solution.shape
    width = trace_matrix.shape[0] // 6
    parts = split(local, elements)
    table = jnp.asarray(spectral_constants(local * insts).reshape(-1))
    vmem = pl.BlockSpec(memory_space=pltpu.VMEM)
    away = pl.BlockSpec(memory_space=pltpu.HBM)
    narrow = jnp.bfloat16
    grant = 67043328 - 2 * solution.size - 65536
    dma = pltpu.SemaphoreType.DMA
    return pl.pallas_call(
        functools.partial(kernel, insts, shards),
        name="sweep",
        out_shape=pltpu.VMEM(solution.shape, narrow),
        in_specs=[vmem] + [away] * 10,
        out_specs=vmem,
        scratch_shapes=[
            pltpu.SMEM(table.shape, jnp.float32),
            pltpu.VMEM(metric_scale.shape, jnp.float32),
            pltpu.VMEM((6, 1, elements), jnp.int32),
            pltpu.VMEM(partner.shape, jnp.int32),
            pltpu.VMEM((local, dof, elements), narrow),
            pltpu.VMEM((local, dof, elements), narrow),
            pltpu.VMEM(volume_matrix.shape, narrow),
            pltpu.VMEM(trace_matrix.shape[::-1], narrow),
            pltpu.VMEM(trace_matrix.shape, narrow),
            pltpu.VMEM(lift_matrix.shape, narrow),
            pltpu.VMEM(block_inverse.shape, narrow),
            pltpu.VMEM((max(insts - 1, 1), local, dof, elements), narrow),
            pltpu.VMEM((6, local * width, elements), narrow),
            pltpu.VMEM((local, 6 * width, elements), narrow),
            pltpu.VMEM((local, dof, elements), jnp.float32),
            pltpu.VMEM((2, 2, local * width, LANES), narrow),
            pltpu.VMEM((shards, local * width, LANES), narrow),
            dma((2,)),
            dma,
            dma((max(insts - 1, 1), len(parts))),
            dma,
            dma,
            pltpu.SemaphoreType.REGULAR,
            pltpu.SemaphoreType.REGULAR,
            pltpu.SemaphoreType.REGULAR,
            pltpu.SemaphoreType.REGULAR,
            pltpu.VMEM((dof, CHUNK), narrow),
            dma,
            pltpu.VMEM((8, LANES), jnp.float32),
            dma,
        ],
        compiler_params=pltpu.CompilerParams(
            collective_id=0, has_side_effects=True, vmem_limit_bytes=grant
        ),
    )(
        lax.cond(
            lax.axis_index("inst") == 0,
            lambda value: jnp.broadcast_to(value, (8, LANES)),
            lambda value: jnp.zeros((8, LANES), jnp.float32),
            frequency,
        ),
        table,
        metric_scale,
        jnp.transpose(adjacency, (1, 0, 2)),
        partner,
        solution,
        forcing,
        volume_matrix,
        trace_matrix.T,
        lift_matrix,
        block_inverse,
    )


def solution(mesh):
    in_specs = (
        P("row", "inst", None, ("groups", "space")),
        P("row", "inst", None, ("groups", "space")),
        P("row", ("groups", "space")),
        P(),
        P("row", None, ("groups", "space")),
        P("row", "inst", ("groups", "space")),
        P(),
        P(),
        P(),
        P(),
    )
    out_specs = P("row", "inst", None, ("groups", "space"))
    return jax.shard_map(body, mesh=mesh, in_specs=in_specs, out_specs=out_specs, check_vma=False)
```

```python
import functools

import jax
import jax.numpy as jnp
import numpy as np
from jax import lax
from jax.experimental import pallas as pl
from jax.experimental.pallas import tpu as pltpu
from jax.sharding import PartitionSpec as P

LAYER = 64
LANES = 128
CHUNK = 128
TILE = 256
OPPOSITE = (1, 0, 3, 2, 5, 4)
MESH = pl.DeviceIdType.MESH


def spectral_constants(instances):
    positions = np.arange(instances)
    distance = (positions[:, None] - positions[None, :]).astype(np.float32)
    parity = (1.0 - 2.0 * np.mod(positions[:, None] + positions[None, :], 2)).astype(np.float32)
    angles = (np.float32(np.pi) * distance / np.float32(instances)).astype(np.float32)
    sine_values = np.where(distance == 0.0, np.float32(1.0), np.sin(angles))
    cotangent = np.where(distance == 0.0, np.float32(0.0), np.cos(angles) / sine_values)
    return (np.float32(0.5) * parity * cotangent).astype(np.float32)


def one_hot(ids, first, rows):
    numbers = lax.broadcasted_iota(jnp.int32, (rows, ids.shape[1]), 0) + first
    return jnp.where(numbers == ids, 1.0, 0.0).astype(jnp.bfloat16)


def mm(a, b):
    return jnp.dot(a, b, preferred_element_type=jnp.float32)


def kernel(
    insts,
    shards,
    given,
    table_hbm,
    scales_hbm,
    adjacency_hbm,
    partner_hbm,
    solution_hbm,
    forcing_hbm,
    volume_hbm,
    trace_hbm,
    lift_hbm,
    inverse_hbm,
    result,
    table,
    scales,
    adjacency,
    partner,
    current,
    forcing,
    volume_matrix,
    trace_turned,
    trace_matrix,
    lift_matrix,
    inverse,
    others,
    traces,
    beside,
    partial,
    halos,
    crossed,
    load_sem,
    sending,
    inst_recv,
    halo_recv,
    cross_recv,
    above,
    ready,
    met,
    opened,
    relayed,
    relay_recv,
    frequency,
    frequency_recv,
):
    local, dof, elements = current.shape
    width = trace_matrix.shape[0] // 6
    iface = partner.shape[2]
    parts = split(local, elements)
    my_inst = lax.axis_index("inst")
    my_space = lax.axis_index("space")
    section = lax.axis_index("row")
    right = lax.rem(my_space + 1, shards)
    left = lax.rem(my_space + shards - 1, shards)

    barrier = pltpu.get_barrier_semaphore()
    def signal(semaphore, target):
        pl.semaphore_signal(semaphore, inc=1, device_id=target, device_id_type=MESH)

    leads = my_inst == 0
    other_row = {"row": 1 - section}
    peers = [{"inst": lax.rem(my_inst + k, insts)} for k in range(1, insts)]
    for peer in peers:
        signal(barrier, peer)

    @pl.when(leads)
    def _():
        signal(barrier, other_row)

    @pl.when(jnp.logical_and(leads, my_space < shards - 1))
    def _():
        signal(barrier, {"space": my_space + 1})

    greeted = jnp.where(leads, 1 + jnp.minimum(my_space, 1), 0)
    pl.semaphore_wait(barrier, insts - 1 + greeted)

    def inst_copy(k, part):
        picked, start, stop = parts[part]
        return pltpu.make_async_remote_copy(
            src_ref=solution_hbm.at[0, picked, :, start:stop],
            dst_ref=others.at[k - 1, picked, :, start:stop],
            send_sem=sending,
            recv_sem=inst_recv.at[k - 1, part],
            device_id={"inst": lax.rem(my_inst + k, insts)},
            device_id_type=MESH,
        )

    early = range(1, 2 + min(local - 1, 1))
    late = range(early.stop, len(parts))

    def send(numbers):
        for part in numbers:
            for k in range(1, insts):
                inst_copy(k, part).start()

    holds = jnp.logical_and(leads, section == 0)

    def share(k):
        return pltpu.make_async_remote_copy(
            src_ref=given,
            dst_ref=frequency,
            send_sem=sending,
            recv_sem=frequency_recv,
            device_id=peers[k - 1],
            device_id_type=MESH,
        )

    @pl.when(holds)
    def _():
        for k in range(1, insts):
            share(k).start()

    @pl.when(section == 0)
    def _():
        send(early)
        send(late)

    @pl.when(section == 1)
    def _():
        send(range(early.stop))

    relay = pltpu.make_async_remote_copy(
        src_ref=solution_hbm.at[0, 0, :, 0:CHUNK],
        dst_ref=relayed,
        send_sem=sending,
        recv_sem=relay_recv,
        device_id=other_row,
        device_id_type=MESH,
    )

    def onward(k):
        return pltpu.make_async_remote_copy(
            src_ref=relayed,
            dst_ref=others.at[k - 1, 0, :, 0:CHUNK],
            send_sem=sending,
            recv_sem=inst_recv.at[k - 1, 0],
            device_id={"inst": lax.rem(my_inst + k, insts), "row": 0},
            device_id_type=MESH,
        )

    loads = []
    for number, (source, target) in enumerate(
        (
            (trace_hbm, trace_turned),
            (solution_hbm.at[0], current),
            (volume_hbm, volume_matrix),
            (lift_hbm, lift_matrix),
            (forcing_hbm.at[0], forcing),
            (inverse_hbm, inverse),
            (adjacency_hbm, adjacency),
            (partner_hbm, partner),
            (scales_hbm, scales),
            (table_hbm, table),
        )
    ):
        copy = pltpu.make_async_copy(source, target, load_sem.at[min(number // 3, 1)])
        copy.start()
        loads.append(copy)

    @pl.when(jnp.logical_and(leads, my_space == shards - 1))
    def _():
        signal(above, {"space": my_space - 1})

    for copy in loads[:3]:
        copy.wait()
    trace_matrix[...] = trace_turned[...].T

    def trace_tile(t, carry):
        columns = pl.ds(pl.multiple_of(t * TILE, TILE), TILE)
        for n in range(local):
            values = mm(trace_matrix[...], current[n, :, columns]).astype(jnp.bfloat16)
            for f in range(6):
                traces[f, n * width : (n + 1) * width, columns] = values[
                    f * width : (f + 1) * width
                ]
        return carry

    lax.fori_loop(0, elements // TILE, trace_tile, 0)

    @pl.when(jnp.logical_and(leads, my_space < shards - 1))
    def _():
        pl.semaphore_wait(above, 1)

    @pl.when(jnp.logical_and(leads, jnp.logical_and(my_space > 0, my_space < shards - 1)))
    def _():
        signal(above, {"space": my_space - 1})

    @pl.when(jnp.logical_and(leads, my_space == 0))
    def _():
        for j in range(1, shards):
            signal(ready, {"space": j})

    def volume_tile(t, carry):
        columns = pl.ds(pl.multiple_of(t * TILE, TILE), TILE)
        for n in range(local):
            partial[n, :, columns] = mm(volume_matrix[...], current[n, :, columns])
        return carry

    lax.fori_loop(0, elements // TILE, volume_tile, 0)

    @pl.when(jnp.logical_and(leads, my_space > 0))
    def _():
        pl.semaphore_wait(ready, 1)

    @pl.when(leads)
    def _():
        signal(met, other_row)
        pl.semaphore_wait(met, 1)
        for peer in peers:
            signal(opened, peer)

    @pl.when(jnp.logical_not(leads))
    def _():
        pl.semaphore_wait(opened, 1)

    across = pltpu.make_async_remote_copy(
        src_ref=frequency,
        dst_ref=frequency,
        send_sem=sending,
        recv_sem=frequency_recv,
        device_id=other_row,
        device_id_type=MESH,
    )

    @pl.when(holds)
    def _():
        frequency[...] = given[...]

    if insts > 1:

        @pl.when(jnp.logical_and(jnp.logical_not(leads), section == 0))
        def _():
            share(1).wait_recv()

    @pl.when(section == 0)
    def _():
        across.start()
        relay.start()

    to_left = pltpu.make_async_remote_copy(
        src_ref=traces.at[4:6, :, 0:LANES],
        dst_ref=halos.at[1],
        send_sem=sending,
        recv_sem=halo_recv,
        device_id={"space": left},
        device_id_type=MESH,
    )
    to_right = pltpu.make_async_remote_copy(
        src_ref=traces.at[4:6, :, elements - LANES : elements],
        dst_ref=halos.at[0],
        send_sem=sending,
        recv_sem=halo_recv,
        device_id={"space": right},
        device_id_type=MESH,
    )
    to_left.start()
    to_right.start()

    def cross_copy(j, slot):
        return pltpu.make_async_remote_copy(
            src_ref=traces.at[1 - section, :, 0:LANES],
            dst_ref=crossed.at[slot],
            send_sem=sending,
            recv_sem=cross_recv,
            device_id={"space": j, "row": 1 - section},
            device_id_type=MESH,
        )

    for j in range(shards):
        cross_copy(j, my_space).start()

    def put(face, columns, values):
        for n in range(local):
            beside[n, face * width : (face + 1) * width, columns] = values[
                n * width : (n + 1) * width
            ].astype(jnp.bfloat16)

    for copy in loads[3:]:
        copy.wait()
    for face in range(6):

        def gather_tile(t, carry, face=face):
            columns = pl.ds(pl.multiple_of(t * TILE, TILE), TILE)
            ids = adjacency[face, :, columns]
            put(face, columns, mm(traces[OPPOSITE[face]], one_hot(ids, LAYER, elements)))
            return carry

        lax.fori_loop(0, elements // TILE, gather_tile, 0)
        if face == 1:

            @pl.when(section == 1)
            def _():
                relay.wait_recv()
                for k in range(1, insts):
                    onward(k).start()
                send(late)

    both = pltpu.make_async_remote_copy(
        src_ref=halos,
        dst_ref=halos,
        send_sem=sending,
        recv_sem=halo_recv,
        device_id={"space": left},
        device_id_type=MESH,
    )
    both.wait_recv()
    ends = (0,) if elements == LANES else (0, elements - LANES)
    for face in (4, 5):
        for start in ends:
            columns = pl.ds(start, LANES)
            ids = adjacency[face, :, columns]
            facing = OPPOSITE[face] - 4
            low = mm(halos[0, facing], one_hot(ids, LAYER - LANES, LANES))
            high = mm(halos[1, facing], one_hot(ids, LAYER + elements, LANES))
            for n in range(local):
                rows = slice(face * width, (face + 1) * width)
                lines = slice(n * width, (n + 1) * width)
                beside[n, rows, columns] = (
                    beside[n, rows, columns].astype(jnp.float32) + low[lines] + high[lines]
                ).astype(jnp.bfloat16)

    every = pltpu.make_async_remote_copy(
        src_ref=crossed,
        dst_ref=crossed,
        send_sem=sending,
        recv_sem=cross_recv,
        device_id={"row": 1 - section},
        device_id_type=MESH,
    )
    every.wait_recv()
    for n in range(local):
        ids = partner[0, n : n + 1, :]
        lines = slice(n * width, (n + 1) * width)
        total = jnp.zeros((width, iface), jnp.float32)
        for j in range(shards):
            hot = one_hot(ids, j * iface, iface)
            total += mm(crossed[j, lines, 0:iface], hot)
        incoming = total.astype(jnp.bfloat16)
        for face in range(2):
            rows = slice(face * width, (face + 1) * width)
            beside[n, rows, 0:iface] = jnp.where(
                section == 1 - face, incoming, beside[n, rows, 0:iface]
            )


    @pl.when(section == 1)
    def _():
        across.wait_recv()

    factor = frequency[0:1, 0:1]
    all_inst = local * insts

    def weight(n, owner, m):
        return factor * table[(my_inst * local + n) * all_inst + owner * local + m]

    def lift_tile(t, carry):
        columns = pl.ds(pl.multiple_of(t * TILE, TILE), TILE)
        scale = scales[:, columns]
        inverse_scale = 1.0 / scale
        for n in range(local):
            coupled = mm(lift_matrix[...], beside[n, :, columns])
            residual = forcing[n, :, columns].astype(jnp.float32) - scale * (
                partial[n, :, columns] + coupled
            )
            for m in range(local):
                residual -= weight(n, my_inst, m) * current[m, :, columns].astype(jnp.float32)
            update = mm(inverse[...], residual.astype(jnp.bfloat16))
            partial[n, :, columns] = (
                current[n, :, columns].astype(jnp.float32) + update * inverse_scale
            )
        return carry

    lax.fori_loop(0, elements // TILE, lift_tile, 0)

    for part, (picked, start, stop) in enumerate(parts):
        chosen = range(local)[picked]
        wide = TILE if (stop - start) % TILE == 0 else CHUNK
        for k in range(1, insts):
            owner = lax.rem(my_inst + insts - k, insts)
            last = k == insts - 1 and chosen[-1] == local - 1
            inst_copy(k, part).wait_recv()

            def turn_tile(t, carry):
                columns = pl.ds(pl.multiple_of(start + t * wide, wide), wide)
                inverse_scale = 1.0 / scales[:, columns]
                values = [partial[n, :, columns] for n in range(local)]
                for m in chosen:
                    update = mm(inverse[...], others[k - 1, m, :, columns]) * inverse_scale
                    values = [values[n] - weight(n, owner, m) * update for n in range(local)]
                for n in range(local):
                    if last:
                        result[0, n, :, columns] = values[n].astype(jnp.bfloat16)
                    else:
                        partial[n, :, columns] = values[n]
                return carry

            lax.fori_loop(0, (stop - start) // wide, turn_tile, 0)

    if insts == 1:
        result[0] = partial[...].astype(jnp.bfloat16)

    both.wait_send()
    every.wait_send()

    def sent(source):
        pltpu.make_async_remote_copy(
            src_ref=source,
            dst_ref=source,
            send_sem=sending,
            recv_sem=relay_recv,
            device_id=other_row,
            device_id_type=MESH,
        ).wait_send()

    @pl.when(holds)
    def _():
        for _ in peers:
            sent(frequency)

    @pl.when(section == 0)
    def _():
        sent(frequency)
        sent(relayed)
        sent(others.at[:, 0, :, CHUNK:])
        if local > 1:
            sent(others.at[:, 1:])

    @pl.when(section == 1)
    def _():
        sent(others.at[:, 0, :, 0:CHUNK])
        sent(others)


def split(local, elements):
    half = elements // (2 * CHUNK) * CHUNK
    parts = [(slice(0, 1), 0, CHUNK), (slice(0, 1), CHUNK, half)]
    if local > 1:
        parts.append((slice(1, local), 0, half))
    start = half
    while elements - start > CHUNK:
        stop = start + max(CHUNK, (elements - start) // (2 * CHUNK) * CHUNK)
        parts.append((slice(0, local), start, stop))
        start = stop
    return parts + [(slice(m, m + 1), start, elements) for m in range(local)]


def body(
    solution,
    forcing,
    metric_scale,
    frequency,
    adjacency,
    partner,
    volume_matrix,
    trace_matrix,
    lift_matrix,
    block_inverse,
):
    insts = lax.axis_size("inst")
    shards = lax.axis_size("space")
    _, local, dof, elements = solution.shape
    width = trace_matrix.shape[0] // 6
    parts = split(local, elements)
    table = jnp.asarray(spectral_constants(local * insts).reshape(-1))
    vmem = pl.BlockSpec(memory_space=pltpu.VMEM)
    away = pl.BlockSpec(memory_space=pltpu.HBM)
    narrow = jnp.bfloat16
    grant = 67043328 - 2 * solution.size - 65536
    dma = pltpu.SemaphoreType.DMA
    return pl.pallas_call(
        functools.partial(kernel, insts, shards),
        name="sweep",
        out_shape=pltpu.VMEM(solution.shape, narrow),
        in_specs=[vmem] + [away] * 10,
        out_specs=vmem,
        scratch_shapes=[
            pltpu.SMEM(table.shape, jnp.float32),
            pltpu.VMEM(metric_scale.shape, jnp.float32),
            pltpu.VMEM((6, 1, elements), jnp.int32),
            pltpu.VMEM(partner.shape, jnp.int32),
            pltpu.VMEM((local, dof, elements), narrow),
            pltpu.VMEM((local, dof, elements), narrow),
            pltpu.VMEM(volume_matrix.shape, narrow),
            pltpu.VMEM(trace_matrix.shape[::-1], narrow),
            pltpu.VMEM(trace_matrix.shape, narrow),
            pltpu.VMEM(lift_matrix.shape, narrow),
            pltpu.VMEM(block_inverse.shape, narrow),
            pltpu.VMEM((max(insts - 1, 1), local, dof, elements), narrow),
            pltpu.VMEM((6, local * width, elements), narrow),
            pltpu.VMEM((local, 6 * width, elements), narrow),
            pltpu.VMEM((local, dof, elements), jnp.float32),
            pltpu.VMEM((2, 2, local * width, LANES), narrow),
            pltpu.VMEM((shards, local * width, LANES), narrow),
            dma((2,)),
            dma,
            dma((max(insts - 1, 1), len(parts))),
            dma,
            dma,
            pltpu.SemaphoreType.REGULAR,
            pltpu.SemaphoreType.REGULAR,
            pltpu.SemaphoreType.REGULAR,
            pltpu.SemaphoreType.REGULAR,
            pltpu.VMEM((dof, CHUNK), narrow),
            dma,
            pltpu.VMEM((8, LANES), jnp.float32),
            dma,
        ],
        compiler_params=pltpu.CompilerParams(
            collective_id=0, has_side_effects=True, vmem_limit_bytes=grant
        ),
    )(
        lax.cond(
            jnp.logical_and(lax.axis_index("inst") == 0, lax.axis_index("row") == 0),
            lambda value: jnp.broadcast_to(value, (8, LANES)),
            lambda value: jnp.zeros((8, LANES), jnp.float32),
            frequency,
        ),
        table,
        metric_scale,
        jnp.transpose(adjacency, (1, 0, 2)),
        partner,
        solution,
        forcing,
        volume_matrix,
        trace_matrix.T,
        lift_matrix,
        block_inverse,
    )


def solution(mesh):
    in_specs = (
        P("row", "inst", None, ("groups", "space")),
        P("row", "inst", None, ("groups", "space")),
        P("row", ("groups", "space")),
        P(),
        P("row", None, ("groups", "space")),
        P("row", "inst", ("groups", "space")),
        P(),
        P(),
        P(),
        P(),
    )
    out_specs = P("row", "inst", None, ("groups", "space"))
    return jax.shard_map(body, mesh=mesh, in_specs=in_specs, out_specs=out_specs, check_vma=False)
```

```python
import functools

import jax
import jax.numpy as jnp
import numpy as np
from jax import lax
from jax.experimental import pallas as pl
from jax.experimental.pallas import tpu as pltpu
from jax.sharding import PartitionSpec as P

LAYER = 64
LANES = 128
CHUNK = 128
TILE = 256
OPPOSITE = (1, 0, 3, 2, 5, 4)
MESH = pl.DeviceIdType.MESH


def spectral_constants(instances):
    positions = np.arange(instances)
    distance = (positions[:, None] - positions[None, :]).astype(np.float32)
    parity = (1.0 - 2.0 * np.mod(positions[:, None] + positions[None, :], 2)).astype(np.float32)
    angles = (np.float32(np.pi) * distance / np.float32(instances)).astype(np.float32)
    sine_values = np.where(distance == 0.0, np.float32(1.0), np.sin(angles))
    cotangent = np.where(distance == 0.0, np.float32(0.0), np.cos(angles) / sine_values)
    return (np.float32(0.5) * parity * cotangent).astype(np.float32)


def one_hot(ids, first, rows):
    numbers = lax.broadcasted_iota(jnp.int32, (rows, ids.shape[1]), 0) + first
    return jnp.where(numbers == ids, 1.0, 0.0).astype(jnp.bfloat16)


def mm(a, b):
    return jnp.dot(a, b, preferred_element_type=jnp.float32)


def kernel(
    insts,
    shards,
    given,
    table_hbm,
    scales_hbm,
    adjacency_hbm,
    partner_hbm,
    solution_hbm,
    forcing_hbm,
    volume_hbm,
    trace_hbm,
    lift_hbm,
    inverse_hbm,
    result,
    table,
    scales,
    adjacency,
    partner,
    current,
    forcing,
    volume_matrix,
    trace_turned,
    trace_matrix,
    lift_matrix,
    inverse,
    others,
    traces,
    beside,
    partial,
    arrived,
    load_sem,
    sending,
    inst_recv,
    spread,
    column,
    plane,
    relayed,
    frequency,
    handed,
    relay_recv,
):
    local, dof, elements = current.shape
    width = trace_matrix.shape[0] // 6
    iface = partner.shape[2]
    parts = split(local, elements)
    my_inst = lax.axis_index("inst")
    my_space = lax.axis_index("space")
    section = lax.axis_index("row")
    right = lax.rem(my_space + 1, shards)
    left = lax.rem(my_space + shards - 1, shards)

    barrier = pltpu.get_barrier_semaphore()
    def signal(semaphore, target):
        pl.semaphore_signal(semaphore, inc=1, device_id=target, device_id_type=MESH)

    leads = my_inst == 0
    other_row = {"row": 1 - section}
    peers = [{"inst": lax.rem(my_inst + k, insts)} for k in range(1, insts)]
    for peer in peers:
        signal(barrier, peer)

    @pl.when(leads)
    def _():
        signal(barrier, other_row)

    @pl.when(jnp.logical_and(leads, my_space < shards - 1))
    def _():
        signal(barrier, {"space": my_space + 1})

    greeted = jnp.where(leads, 1 + jnp.minimum(my_space, 1), 0)
    pl.semaphore_wait(barrier, insts - 1 + greeted)

    early = range(1, 2 + min(local - 1, 1))
    late = range(early.stop, len(parts))

    def inst_copy(k, part):
        picked, start, stop = parts[part]
        return pltpu.make_async_remote_copy(
            src_ref=solution_hbm.at[0, picked, :, start:stop],
            dst_ref=others.at[k - 1, picked, :, start:stop],
            send_sem=sending,
            recv_sem=inst_recv.at[k - 1, max(part - early.stop + 1, 0)],
            device_id={"inst": lax.rem(my_inst + k, insts)},
            device_id_type=MESH,
        )


    def send(numbers):
        for part in numbers:
            for k in range(1, insts):
                inst_copy(k, part).start()

    holds = jnp.logical_and(leads, section == 0)

    def share(k):
        return pltpu.make_async_remote_copy(
            src_ref=given,
            dst_ref=frequency,
            send_sem=sending,
            recv_sem=handed,
            device_id=peers[k - 1],
            device_id_type=MESH,
        )

    @pl.when(holds)
    def _():
        for k in range(1, insts):
            share(k).start()

    @pl.when(section == 0)
    def _():
        send(early)
        send(late)

    @pl.when(section == 1)
    def _():
        send(range(early.stop))

    relay = pltpu.make_async_remote_copy(
        src_ref=solution_hbm.at[0, 0, :, 0:CHUNK],
        dst_ref=relayed,
        send_sem=sending,
        recv_sem=relay_recv,
        device_id=other_row,
        device_id_type=MESH,
    )

    def onward(k):
        return pltpu.make_async_remote_copy(
            src_ref=relayed,
            dst_ref=others.at[k - 1, 0, :, 0:CHUNK],
            send_sem=sending,
            recv_sem=inst_recv.at[k - 1, 0],
            device_id={"inst": lax.rem(my_inst + k, insts), "row": 0},
            device_id_type=MESH,
        )

    loads = []
    for number, (source, target) in enumerate(
        (
            (trace_hbm, trace_turned),
            (solution_hbm.at[0], current),
            (volume_hbm, volume_matrix),
            (lift_hbm, lift_matrix),
            (forcing_hbm.at[0], forcing),
            (inverse_hbm, inverse),
            (adjacency_hbm, adjacency),
            (partner_hbm, partner),
            (scales_hbm, scales),
            (table_hbm, table),
        )
    ):
        copy = pltpu.make_async_copy(source, target, load_sem.at[min(number // 3, 1)])
        copy.start()
        loads.append(copy)

    @pl.when(jnp.logical_and(leads, my_space == shards - 1))
    def _():
        signal(column, {"space": my_space - 1})

    for copy in loads[:3]:
        copy.wait()
    trace_matrix[...] = trace_turned[...].T

    def trace_tile(t, carry):
        columns = pl.ds(pl.multiple_of(t * TILE, TILE), TILE)
        for n in range(local):
            values = mm(trace_matrix[...], current[n, :, columns]).astype(jnp.bfloat16)
            for f in range(6):
                traces[f, n * width : (n + 1) * width, columns] = values[
                    f * width : (f + 1) * width
                ]
        return carry

    lax.fori_loop(0, elements // TILE, trace_tile, 0)

    @pl.when(jnp.logical_and(leads, my_space < shards - 1))
    def _():
        pl.semaphore_wait(column, 1)

    @pl.when(jnp.logical_and(leads, jnp.logical_and(my_space > 0, my_space < shards - 1)))
    def _():
        signal(column, {"space": my_space - 1})

    @pl.when(jnp.logical_and(leads, my_space == 0))
    def _():
        for j in range(1, shards):
            signal(column, {"space": j})

    def volume_tile(t, carry):
        columns = pl.ds(pl.multiple_of(t * TILE, TILE), TILE)
        for n in range(local):
            partial[n, :, columns] = mm(volume_matrix[...], current[n, :, columns])
        return carry

    lax.fori_loop(0, elements // TILE, volume_tile, 0)

    @pl.when(jnp.logical_and(leads, my_space > 0))
    def _():
        pl.semaphore_wait(column, 1)

    @pl.when(leads)
    def _():
        signal(plane, other_row)
        pl.semaphore_wait(plane, 1)
        for peer in peers:
            signal(plane, peer)

    @pl.when(jnp.logical_not(leads))
    def _():
        pl.semaphore_wait(plane, 1)

    across = pltpu.make_async_remote_copy(
        src_ref=frequency,
        dst_ref=frequency,
        send_sem=sending,
        recv_sem=handed,
        device_id=other_row,
        device_id_type=MESH,
    )

    @pl.when(holds)
    def _():
        frequency[...] = given[...]

    if insts > 1:

        @pl.when(jnp.logical_and(jnp.logical_not(leads), section == 0))
        def _():
            share(1).wait_recv()

    @pl.when(section == 0)
    def _():
        across.start()
        relay.start()

    to_left = pltpu.make_async_remote_copy(
        src_ref=traces.at[4:6, :, 0:LANES],
        dst_ref=arrived.at[2:4],
        send_sem=sending,
        recv_sem=spread,
        device_id={"space": left},
        device_id_type=MESH,
    )
    to_right = pltpu.make_async_remote_copy(
        src_ref=traces.at[4:6, :, elements - LANES : elements],
        dst_ref=arrived.at[0:2],
        send_sem=sending,
        recv_sem=spread,
        device_id={"space": right},
        device_id_type=MESH,
    )
    to_left.start()
    to_right.start()

    def cross_copy(j, slot):
        return pltpu.make_async_remote_copy(
            src_ref=traces.at[1 - section, :, 0:LANES],
            dst_ref=arrived.at[4 + slot],
            send_sem=sending,
            recv_sem=spread,
            device_id={"space": j, "row": 1 - section},
            device_id_type=MESH,
        )

    for j in range(shards):
        cross_copy(j, my_space).start()

    def put(face, columns, values):
        for n in range(local):
            beside[n, face * width : (face + 1) * width, columns] = values[
                n * width : (n + 1) * width
            ].astype(jnp.bfloat16)

    for copy in loads[3:]:
        copy.wait()
    for face in range(6):

        def gather_tile(t, carry, face=face):
            columns = pl.ds(pl.multiple_of(t * TILE, TILE), TILE)
            ids = adjacency[face, :, columns]
            put(face, columns, mm(traces[OPPOSITE[face]], one_hot(ids, LAYER, elements)))
            return carry

        lax.fori_loop(0, elements // TILE, gather_tile, 0)
        if face == 1:

            @pl.when(section == 1)
            def _():
                relay.wait_recv()
                across.wait_recv()
                for k in range(1, insts):
                    onward(k).start()
                send(late)

    every = pltpu.make_async_remote_copy(
        src_ref=arrived,
        dst_ref=arrived,
        send_sem=sending,
        recv_sem=spread,
        device_id=other_row,
        device_id_type=MESH,
    )
    every.wait_recv()
    ends = (0,) if elements == LANES else (0, elements - LANES)
    for face in (4, 5):
        for start in ends:
            columns = pl.ds(start, LANES)
            ids = adjacency[face, :, columns]
            facing = OPPOSITE[face] - 4
            low = mm(arrived[facing], one_hot(ids, LAYER - LANES, LANES))
            high = mm(arrived[2 + facing], one_hot(ids, LAYER + elements, LANES))
            for n in range(local):
                rows = slice(face * width, (face + 1) * width)
                lines = slice(n * width, (n + 1) * width)
                beside[n, rows, columns] = (
                    beside[n, rows, columns].astype(jnp.float32) + low[lines] + high[lines]
                ).astype(jnp.bfloat16)

    for n in range(local):
        ids = partner[0, n : n + 1, :]
        lines = slice(n * width, (n + 1) * width)
        total = jnp.zeros((width, iface), jnp.float32)
        for j in range(shards):
            hot = one_hot(ids, j * iface, iface)
            total += mm(arrived[4 + j, lines, 0:iface], hot)
        incoming = total.astype(jnp.bfloat16)
        for face in range(2):
            rows = slice(face * width, (face + 1) * width)
            beside[n, rows, 0:iface] = jnp.where(
                section == 1 - face, incoming, beside[n, rows, 0:iface]
            )


    factor = frequency[0:1, 0:1]
    all_inst = local * insts

    def weight(n, owner, m):
        return factor * table[(my_inst * local + n) * all_inst + owner * local + m]

    def lift_tile(t, carry):
        columns = pl.ds(pl.multiple_of(t * TILE, TILE), TILE)
        scale = scales[:, columns]
        inverse_scale = 1.0 / scale
        for n in range(local):
            coupled = mm(lift_matrix[...], beside[n, :, columns])
            residual = forcing[n, :, columns].astype(jnp.float32) - scale * (
                partial[n, :, columns] + coupled
            )
            for m in range(local):
                residual -= weight(n, my_inst, m) * current[m, :, columns].astype(jnp.float32)
            update = mm(inverse[...], residual.astype(jnp.bfloat16))
            partial[n, :, columns] = (
                current[n, :, columns].astype(jnp.float32) + update * inverse_scale
            )
        return carry

    lax.fori_loop(0, elements // TILE, lift_tile, 0)

    def first_half(k):
        block = others.at[k - 1, :, :, 0 : parts[early.stop][1]]
        return pltpu.make_async_remote_copy(
            src_ref=block,
            dst_ref=block,
            send_sem=sending,
            recv_sem=inst_recv.at[k - 1, 0],
            device_id=peers[k - 1],
            device_id_type=MESH,
        )

    for part, (picked, start, stop) in enumerate(parts):
        chosen = range(local)[picked]
        wide = TILE if (stop - start) % TILE == 0 else CHUNK
        for k in range(1, insts):
            owner = lax.rem(my_inst + insts - k, insts)
            last = k == insts - 1 and chosen[-1] == local - 1
            if part == 0:
                first_half(k).wait_recv()
            elif part >= early.stop:
                inst_copy(k, part).wait_recv()

            def turn_tile(t, carry):
                columns = pl.ds(pl.multiple_of(start + t * wide, wide), wide)
                inverse_scale = 1.0 / scales[:, columns]
                values = [partial[n, :, columns] for n in range(local)]
                for m in chosen:
                    update = mm(inverse[...], others[k - 1, m, :, columns]) * inverse_scale
                    values = [values[n] - weight(n, owner, m) * update for n in range(local)]
                for n in range(local):
                    if last:
                        result[0, n, :, columns] = values[n].astype(jnp.bfloat16)
                    else:
                        partial[n, :, columns] = values[n]
                return carry

            lax.fori_loop(0, (stop - start) // wide, turn_tile, 0)

    if insts == 1:
        result[0] = partial[...].astype(jnp.bfloat16)

    every.wait_send()

    def sent(source):
        pltpu.make_async_remote_copy(
            src_ref=source,
            dst_ref=source,
            send_sem=sending,
            recv_sem=handed,
            device_id=other_row,
            device_id_type=MESH,
        ).wait_send()

    @pl.when(holds)
    def _():
        for _ in peers:
            sent(frequency)

    @pl.when(section == 0)
    def _():
        sent(frequency)
        sent(relayed)
        sent(others.at[:, 0, :, CHUNK:])
        if local > 1:
            sent(others.at[:, 1:])

    @pl.when(section == 1)
    def _():
        sent(others.at[:, 0, :, 0:CHUNK])
        sent(others)


def split(local, elements):
    half = elements // (2 * CHUNK) * CHUNK
    parts = [(slice(0, 1), 0, CHUNK), (slice(0, 1), CHUNK, half)]
    if local > 1:
        parts.append((slice(1, local), 0, half))
    start = half
    while elements - start > CHUNK:
        stop = start + max(CHUNK, (elements - start) // (2 * CHUNK) * CHUNK)
        parts.append((slice(0, local), start, stop))
        start = stop
    return parts + [(slice(m, m + 1), start, elements) for m in range(local)]


def body(
    solution,
    forcing,
    metric_scale,
    frequency,
    adjacency,
    partner,
    volume_matrix,
    trace_matrix,
    lift_matrix,
    block_inverse,
):
    insts = lax.axis_size("inst")
    shards = lax.axis_size("space")
    _, local, dof, elements = solution.shape
    width = trace_matrix.shape[0] // 6
    parts = split(local, elements)
    table = jnp.asarray(spectral_constants(local * insts).reshape(-1))
    vmem = pl.BlockSpec(memory_space=pltpu.VMEM)
    away = pl.BlockSpec(memory_space=pltpu.HBM)
    narrow = jnp.bfloat16
    grant = 67043328 - 2 * solution.size - 65536
    dma = pltpu.SemaphoreType.DMA
    return pl.pallas_call(
        functools.partial(kernel, insts, shards),
        name="sweep",
        out_shape=pltpu.VMEM(solution.shape, narrow),
        in_specs=[vmem] + [away] * 10,
        out_specs=vmem,
        scratch_shapes=[
            pltpu.SMEM(table.shape, jnp.float32),
            pltpu.VMEM(metric_scale.shape, jnp.float32),
            pltpu.VMEM((6, 1, elements), jnp.int32),
            pltpu.VMEM(partner.shape, jnp.int32),
            pltpu.VMEM((local, dof, elements), narrow),
            pltpu.VMEM((local, dof, elements), narrow),
            pltpu.VMEM(volume_matrix.shape, narrow),
            pltpu.VMEM(trace_matrix.shape[::-1], narrow),
            pltpu.VMEM(trace_matrix.shape, narrow),
            pltpu.VMEM(lift_matrix.shape, narrow),
            pltpu.VMEM(block_inverse.shape, narrow),
            pltpu.VMEM((max(insts - 1, 1), local, dof, elements), narrow),
            pltpu.VMEM((6, local * width, elements), narrow),
            pltpu.VMEM((local, 6 * width, elements), narrow),
            pltpu.VMEM((local, dof, elements), jnp.float32),
            pltpu.VMEM((4 + shards, local * width, LANES), narrow),
            dma((2,)),
            dma,
            dma((max(insts - 1, 1), len(parts) - min(local - 1, 1) - 1)),
            dma,
            pltpu.SemaphoreType.REGULAR,
            pltpu.SemaphoreType.REGULAR,
            pltpu.VMEM((dof, CHUNK), narrow),
            pltpu.VMEM((8, LANES), jnp.float32),
            dma,
            dma,
        ],
        compiler_params=pltpu.CompilerParams(
            collective_id=0, has_side_effects=True, vmem_limit_bytes=grant
        ),
    )(
        lax.cond(
            jnp.logical_and(lax.axis_index("inst") == 0, lax.axis_index("row") == 0),
            lambda value: jnp.broadcast_to(value, (8, LANES)),
            lambda value: jnp.zeros((8, LANES), jnp.float32),
            frequency,
        ),
        table,
        metric_scale,
        jnp.transpose(adjacency, (1, 0, 2)),
        partner,
        solution,
        forcing,
        volume_matrix,
        trace_matrix.T,
        lift_matrix,
        block_inverse,
    )


def solution(mesh):
    in_specs = (
        P("row", "inst", None, ("groups", "space")),
        P("row", "inst", None, ("groups", "space")),
        P("row", ("groups", "space")),
        P(),
        P("row", None, ("groups", "space")),
        P("row", "inst", ("groups", "space")),
        P(),
        P(),
        P(),
        P(),
    )
    out_specs = P("row", "inst", None, ("groups", "space"))
    return jax.shard_map(body, mesh=mesh, in_specs=in_specs, out_specs=out_specs, check_vma=False)
```

```python
import functools

import jax
import jax.numpy as jnp
import numpy as np
from jax import lax
from jax.experimental import pallas as pl
from jax.experimental.pallas import tpu as pltpu
from jax.sharding import PartitionSpec as P

LAYER = 64
LANES = 128
CHUNK = 128
TILE = 256
OPPOSITE = (1, 0, 3, 2, 5, 4)
MESH = pl.DeviceIdType.MESH


def spectral_constants(instances):
    positions = np.arange(instances)
    distance = (positions[:, None] - positions[None, :]).astype(np.float32)
    parity = (1.0 - 2.0 * np.mod(positions[:, None] + positions[None, :], 2)).astype(np.float32)
    angles = (np.float32(np.pi) * distance / np.float32(instances)).astype(np.float32)
    sine_values = np.where(distance == 0.0, np.float32(1.0), np.sin(angles))
    cotangent = np.where(distance == 0.0, np.float32(0.0), np.cos(angles) / sine_values)
    return (np.float32(0.5) * parity * cotangent).astype(np.float32)


def one_hot(ids, first, rows):
    numbers = lax.broadcasted_iota(jnp.int32, (rows, ids.shape[1]), 0) + first
    return jnp.where(numbers == ids, 1.0, 0.0).astype(jnp.bfloat16)


def mm(a, b):
    return jnp.dot(a, b, preferred_element_type=jnp.float32)


def kernel(
    insts,
    shards,
    given,
    table_hbm,
    scales_hbm,
    adjacency_hbm,
    partner_hbm,
    solution_hbm,
    forcing_hbm,
    volume_hbm,
    trace_hbm,
    lift_hbm,
    inverse_hbm,
    result,
    table,
    scales,
    adjacency,
    partner,
    current,
    forcing,
    volume_matrix,
    trace_turned,
    trace_matrix,
    lift_matrix,
    inverse,
    others,
    traces,
    beside,
    partial,
    arrived,
    load_sem,
    sending,
    inst_recv,
    spread,
    column,
    plane,
    relayed,
    frequency,
    handed,
    relay_recv,
):
    local, dof, elements = current.shape
    width = trace_matrix.shape[0] // 6
    iface = partner.shape[2]
    parts = split(local, elements)
    my_inst = lax.axis_index("inst")
    my_space = lax.axis_index("space")
    section = lax.axis_index("row")
    right = lax.rem(my_space + 1, shards)
    left = lax.rem(my_space + shards - 1, shards)

    barrier = pltpu.get_barrier_semaphore()
    def signal(semaphore, target):
        pl.semaphore_signal(semaphore, inc=1, device_id=target, device_id_type=MESH)

    leads = my_inst == 0
    other_row = {"row": 1 - section}
    peers = [{"inst": lax.rem(my_inst + k, insts)} for k in range(1, insts)]
    for peer in peers:
        signal(barrier, peer)

    @pl.when(leads)
    def _():
        signal(barrier, other_row)

    @pl.when(jnp.logical_and(leads, my_space < shards - 1))
    def _():
        signal(barrier, {"space": my_space + 1})

    greeted = jnp.where(leads, 1 + jnp.minimum(my_space, 1), 0)
    pl.semaphore_wait(barrier, insts - 1 + greeted)

    early = range(1, 2 + min(local - 1, 1))
    late = range(early.stop, len(parts))

    def inst_copy(k, part):
        picked, start, stop = parts[part]
        return pltpu.make_async_remote_copy(
            src_ref=solution_hbm.at[0, picked, :, start:stop],
            dst_ref=others.at[k - 1, picked, :, start:stop],
            send_sem=sending,
            recv_sem=inst_recv.at[k - 1, max(part - early.stop + 1, 0)],
            device_id={"inst": lax.rem(my_inst + k, insts)},
            device_id_type=MESH,
        )


    def send(numbers):
        for part in numbers:
            for k in range(1, insts):
                inst_copy(k, part).start()

    holds = jnp.logical_and(leads, section == 0)

    def share(k):
        return pltpu.make_async_remote_copy(
            src_ref=given,
            dst_ref=frequency,
            send_sem=sending,
            recv_sem=handed,
            device_id=peers[k - 1],
            device_id_type=MESH,
        )

    @pl.when(holds)
    def _():
        for k in range(1, insts):
            share(k).start()

    @pl.when(section == 0)
    def _():
        send(early)
        send(late)

    @pl.when(section == 1)
    def _():
        send(range(early.stop))

    final = len(parts) - 1

    def relay(part):
        picked, start, stop = parts[part]
        return pltpu.make_async_remote_copy(
            src_ref=solution_hbm.at[0, picked.start, :, start:stop],
            dst_ref=relayed,
            send_sem=sending,
            recv_sem=relay_recv,
            device_id=other_row,
            device_id_type=MESH,
        )

    def onward(k, part, row):
        picked, start, stop = parts[part]
        return pltpu.make_async_remote_copy(
            src_ref=relayed,
            dst_ref=others.at[k - 1, picked.start, :, start:stop],
            send_sem=sending,
            recv_sem=inst_recv.at[k - 1, max(part - early.stop + 1, 0)],
            device_id={"inst": lax.rem(my_inst + k, insts), "row": row},
            device_id_type=MESH,
        )

    loads = []
    for number, (source, target) in enumerate(
        (
            (trace_hbm, trace_turned),
            (solution_hbm.at[0], current),
            (volume_hbm, volume_matrix),
            (lift_hbm, lift_matrix),
            (forcing_hbm.at[0], forcing),
            (inverse_hbm, inverse),
            (adjacency_hbm, adjacency),
            (partner_hbm, partner),
            (scales_hbm, scales),
            (table_hbm, table),
        )
    ):
        copy = pltpu.make_async_copy(source, target, load_sem.at[min(number // 3, 1)])
        copy.start()
        loads.append(copy)

    @pl.when(jnp.logical_and(leads, my_space == shards - 1))
    def _():
        signal(column, {"space": my_space - 1})

    for copy in loads[:3]:
        copy.wait()
    trace_matrix[...] = trace_turned[...].T

    def trace_tile(t, carry):
        columns = pl.ds(pl.multiple_of(t * TILE, TILE), TILE)
        for n in range(local):
            values = mm(trace_matrix[...], current[n, :, columns]).astype(jnp.bfloat16)
            for f in range(6):
                traces[f, n * width : (n + 1) * width, columns] = values[
                    f * width : (f + 1) * width
                ]
        return carry

    lax.fori_loop(0, elements // TILE, trace_tile, 0)

    @pl.when(jnp.logical_and(leads, my_space < shards - 1))
    def _():
        pl.semaphore_wait(column, 1)

    @pl.when(jnp.logical_and(leads, jnp.logical_and(my_space > 0, my_space < shards - 1)))
    def _():
        signal(column, {"space": my_space - 1})

    @pl.when(jnp.logical_and(leads, my_space == 0))
    def _():
        for j in range(1, shards):
            signal(column, {"space": j})

    def volume_tile(t, carry):
        columns = pl.ds(pl.multiple_of(t * TILE, TILE), TILE)
        for n in range(local):
            partial[n, :, columns] = mm(volume_matrix[...], current[n, :, columns])
        return carry

    lax.fori_loop(0, elements // TILE, volume_tile, 0)

    @pl.when(jnp.logical_and(leads, my_space > 0))
    def _():
        pl.semaphore_wait(column, 1)

    @pl.when(leads)
    def _():
        signal(plane, other_row)
        pl.semaphore_wait(plane, 1)
        for peer in peers:
            signal(plane, peer)

    @pl.when(jnp.logical_not(leads))
    def _():
        pl.semaphore_wait(plane, 1)

    across = pltpu.make_async_remote_copy(
        src_ref=frequency,
        dst_ref=frequency,
        send_sem=sending,
        recv_sem=handed,
        device_id=other_row,
        device_id_type=MESH,
    )

    @pl.when(holds)
    def _():
        frequency[...] = given[...]

    if insts > 1:

        @pl.when(jnp.logical_and(jnp.logical_not(leads), section == 0))
        def _():
            share(1).wait_recv()

    @pl.when(section == 0)
    def _():
        across.start()
        relay(0).start()

    @pl.when(section == 1)
    def _():
        relay(final).start()

    to_left = pltpu.make_async_remote_copy(
        src_ref=traces.at[4:6, :, 0:LANES],
        dst_ref=arrived.at[2:4],
        send_sem=sending,
        recv_sem=spread,
        device_id={"space": left},
        device_id_type=MESH,
    )
    to_right = pltpu.make_async_remote_copy(
        src_ref=traces.at[4:6, :, elements - LANES : elements],
        dst_ref=arrived.at[0:2],
        send_sem=sending,
        recv_sem=spread,
        device_id={"space": right},
        device_id_type=MESH,
    )
    to_left.start()
    to_right.start()

    def cross_copy(j, slot):
        return pltpu.make_async_remote_copy(
            src_ref=traces.at[1 - section, :, 0:LANES],
            dst_ref=arrived.at[4 + slot],
            send_sem=sending,
            recv_sem=spread,
            device_id={"space": j, "row": 1 - section},
            device_id_type=MESH,
        )

    for j in range(shards):
        cross_copy(j, my_space).start()

    def put(face, columns, values):
        for n in range(local):
            beside[n, face * width : (face + 1) * width, columns] = values[
                n * width : (n + 1) * width
            ].astype(jnp.bfloat16)

    for copy in loads[3:]:
        copy.wait()
    for face in range(6):

        def gather_tile(t, carry, face=face):
            columns = pl.ds(pl.multiple_of(t * TILE, TILE), TILE)
            ids = adjacency[face, :, columns]
            put(face, columns, mm(traces[OPPOSITE[face]], one_hot(ids, LAYER, elements)))
            return carry

        lax.fori_loop(0, elements // TILE, gather_tile, 0)
        if face == 1:

            relay(0).wait_recv()

            @pl.when(section == 0)
            def _():
                for k in range(1, insts):
                    onward(k, final, 1).start()

            @pl.when(section == 1)
            def _():
                across.wait_recv()
                for k in range(1, insts):
                    onward(k, 0, 0).start()
                send(late[:-1])

    every = pltpu.make_async_remote_copy(
        src_ref=arrived,
        dst_ref=arrived,
        send_sem=sending,
        recv_sem=spread,
        device_id=other_row,
        device_id_type=MESH,
    )
    every.wait_recv()
    ends = (0,) if elements == LANES else (0, elements - LANES)
    for face in (4, 5):
        for start in ends:
            columns = pl.ds(start, LANES)
            ids = adjacency[face, :, columns]
            facing = OPPOSITE[face] - 4
            low = mm(arrived[facing], one_hot(ids, LAYER - LANES, LANES))
            high = mm(arrived[2 + facing], one_hot(ids, LAYER + elements, LANES))
            for n in range(local):
                rows = slice(face * width, (face + 1) * width)
                lines = slice(n * width, (n + 1) * width)
                beside[n, rows, columns] = (
                    beside[n, rows, columns].astype(jnp.float32) + low[lines] + high[lines]
                ).astype(jnp.bfloat16)

    for n in range(local):
        ids = partner[0, n : n + 1, :]
        lines = slice(n * width, (n + 1) * width)
        total = jnp.zeros((width, iface), jnp.float32)
        for j in range(shards):
            hot = one_hot(ids, j * iface, iface)
            total += mm(arrived[4 + j, lines, 0:iface], hot)
        incoming = total.astype(jnp.bfloat16)
        for face in range(2):
            rows = slice(face * width, (face + 1) * width)
            beside[n, rows, 0:iface] = jnp.where(
                section == 1 - face, incoming, beside[n, rows, 0:iface]
            )


    factor = frequency[0:1, 0:1]
    all_inst = local * insts

    def weight(n, owner, m):
        return factor * table[(my_inst * local + n) * all_inst + owner * local + m]

    def lift_tile(t, carry):
        columns = pl.ds(pl.multiple_of(t * TILE, TILE), TILE)
        scale = scales[:, columns]
        inverse_scale = 1.0 / scale
        for n in range(local):
            coupled = mm(lift_matrix[...], beside[n, :, columns])
            residual = forcing[n, :, columns].astype(jnp.float32) - scale * (
                partial[n, :, columns] + coupled
            )
            for m in range(local):
                residual -= weight(n, my_inst, m) * current[m, :, columns].astype(jnp.float32)
            update = mm(inverse[...], residual.astype(jnp.bfloat16))
            partial[n, :, columns] = (
                current[n, :, columns].astype(jnp.float32) + update * inverse_scale
            )
        return carry

    lax.fori_loop(0, elements // TILE, lift_tile, 0)

    def first_half(k):
        block = others.at[k - 1, :, :, 0 : parts[early.stop][1]]
        return pltpu.make_async_remote_copy(
            src_ref=block,
            dst_ref=block,
            send_sem=sending,
            recv_sem=inst_recv.at[k - 1, 0],
            device_id=peers[k - 1],
            device_id_type=MESH,
        )

    for part, (picked, start, stop) in enumerate(parts):
        chosen = range(local)[picked]
        wide = TILE if (stop - start) % TILE == 0 else CHUNK
        for k in range(1, insts):
            owner = lax.rem(my_inst + insts - k, insts)
            last = k == insts - 1 and chosen[-1] == local - 1
            if part == 0:
                first_half(k).wait_recv()
            elif part >= early.stop:
                inst_copy(k, part).wait_recv()

            def turn_tile(t, carry):
                columns = pl.ds(pl.multiple_of(start + t * wide, wide), wide)
                inverse_scale = 1.0 / scales[:, columns]
                values = [partial[n, :, columns] for n in range(local)]
                for m in chosen:
                    update = mm(inverse[...], others[k - 1, m, :, columns]) * inverse_scale
                    values = [values[n] - weight(n, owner, m) * update for n in range(local)]
                for n in range(local):
                    if last:
                        result[0, n, :, columns] = values[n].astype(jnp.bfloat16)
                    else:
                        partial[n, :, columns] = values[n]
                return carry

            lax.fori_loop(0, (stop - start) // wide, turn_tile, 0)

    if insts == 1:
        result[0] = partial[...].astype(jnp.bfloat16)

    every.wait_send()

    def sent(source):
        pltpu.make_async_remote_copy(
            src_ref=source,
            dst_ref=source,
            send_sem=sending,
            recv_sem=handed,
            device_id=other_row,
            device_id_type=MESH,
        ).wait_send()

    @pl.when(holds)
    def _():
        for _ in peers:
            sent(frequency)

    @pl.when(section == 0)
    def _():
        sent(frequency)

    sent(relayed)
    sent(others)


def split(local, elements):
    half = elements // (2 * CHUNK) * CHUNK
    parts = [(slice(0, 1), 0, CHUNK), (slice(0, 1), CHUNK, half)]
    if local > 1:
        parts.append((slice(1, local), 0, half))
    start = half
    while elements - start > CHUNK:
        stop = start + max(CHUNK, (elements - start) // (2 * CHUNK) * CHUNK)
        parts.append((slice(0, local), start, stop))
        start = stop
    return parts + [(slice(m, m + 1), start, elements) for m in range(local)]


def body(
    solution,
    forcing,
    metric_scale,
    frequency,
    adjacency,
    partner,
    volume_matrix,
    trace_matrix,
    lift_matrix,
    block_inverse,
):
    insts = lax.axis_size("inst")
    shards = lax.axis_size("space")
    _, local, dof, elements = solution.shape
    width = trace_matrix.shape[0] // 6
    parts = split(local, elements)
    table = jnp.asarray(spectral_constants(local * insts).reshape(-1))
    vmem = pl.BlockSpec(memory_space=pltpu.VMEM)
    away = pl.BlockSpec(memory_space=pltpu.HBM)
    narrow = jnp.bfloat16
    grant = 67043328 - 2 * solution.size - 65536
    dma = pltpu.SemaphoreType.DMA
    return pl.pallas_call(
        functools.partial(kernel, insts, shards),
        name="sweep",
        out_shape=pltpu.VMEM(solution.shape, narrow),
        in_specs=[vmem] + [away] * 10,
        out_specs=vmem,
        scratch_shapes=[
            pltpu.SMEM(table.shape, jnp.float32),
            pltpu.VMEM(metric_scale.shape, jnp.float32),
            pltpu.VMEM((6, 1, elements), jnp.int32),
            pltpu.VMEM(partner.shape, jnp.int32),
            pltpu.VMEM((local, dof, elements), narrow),
            pltpu.VMEM((local, dof, elements), narrow),
            pltpu.VMEM(volume_matrix.shape, narrow),
            pltpu.VMEM(trace_matrix.shape[::-1], narrow),
            pltpu.VMEM(trace_matrix.shape, narrow),
            pltpu.VMEM(lift_matrix.shape, narrow),
            pltpu.VMEM(block_inverse.shape, narrow),
            pltpu.VMEM((max(insts - 1, 1), local, dof, elements), narrow),
            pltpu.VMEM((6, local * width, elements), narrow),
            pltpu.VMEM((local, 6 * width, elements), narrow),
            pltpu.VMEM((local, dof, elements), jnp.float32),
            pltpu.VMEM((4 + shards, local * width, LANES), narrow),
            dma((2,)),
            dma,
            dma((max(insts - 1, 1), len(parts) - min(local - 1, 1) - 1)),
            dma,
            pltpu.SemaphoreType.REGULAR,
            pltpu.SemaphoreType.REGULAR,
            pltpu.VMEM((dof, CHUNK), narrow),
            pltpu.VMEM((8, LANES), jnp.float32),
            dma,
            dma,
        ],
        compiler_params=pltpu.CompilerParams(
            collective_id=0, has_side_effects=True, vmem_limit_bytes=grant
        ),
    )(
        lax.cond(
            jnp.logical_and(lax.axis_index("inst") == 0, lax.axis_index("row") == 0),
            lambda value: jnp.broadcast_to(value, (8, LANES)),
            lambda value: jnp.zeros((8, LANES), jnp.float32),
            frequency,
        ),
        table,
        metric_scale,
        jnp.transpose(adjacency, (1, 0, 2)),
        partner,
        solution,
        forcing,
        volume_matrix,
        trace_matrix.T,
        lift_matrix,
        block_inverse,
    )


def solution(mesh):
    in_specs = (
        P("row", "inst", None, ("groups", "space")),
        P("row", "inst", None, ("groups", "space")),
        P("row", ("groups", "space")),
        P(),
        P("row", None, ("groups", "space")),
        P("row", "inst", ("groups", "space")),
        P(),
        P(),
        P(),
        P(),
    )
    out_specs = P("row", "inst", None, ("groups", "space"))
    return jax.shard_map(body, mesh=mesh, in_specs=in_specs, out_specs=out_specs, check_vma=False)
```

```python
import functools

import jax
import jax.numpy as jnp
import numpy as np
from jax import lax
from jax.experimental import pallas as pl
from jax.experimental.pallas import tpu as pltpu
from jax.sharding import PartitionSpec as P

LAYER = 64
LANES = 128
CHUNK = 128
TILE = 256
OPPOSITE = (1, 0, 3, 2, 5, 4)
MESH = pl.DeviceIdType.MESH


def spectral_constants(instances):
    positions = np.arange(instances)
    distance = (positions[:, None] - positions[None, :]).astype(np.float32)
    parity = (1.0 - 2.0 * np.mod(positions[:, None] + positions[None, :], 2)).astype(np.float32)
    angles = (np.float32(np.pi) * distance / np.float32(instances)).astype(np.float32)
    sine_values = np.where(distance == 0.0, np.float32(1.0), np.sin(angles))
    cotangent = np.where(distance == 0.0, np.float32(0.0), np.cos(angles) / sine_values)
    return (np.float32(0.5) * parity * cotangent).astype(np.float32)


def one_hot(ids, first, rows):
    numbers = lax.broadcasted_iota(jnp.int32, (rows, ids.shape[1]), 0) + first
    return jnp.where(numbers == ids, 1.0, 0.0).astype(jnp.bfloat16)


def mm(a, b):
    return jnp.dot(a, b, preferred_element_type=jnp.float32)


def kernel(
    insts,
    shards,
    given,
    table_hbm,
    scales_hbm,
    adjacency_hbm,
    partner_hbm,
    solution_hbm,
    forcing_hbm,
    volume_hbm,
    trace_hbm,
    lift_hbm,
    inverse_hbm,
    result,
    table,
    scales,
    adjacency,
    partner,
    current,
    forcing,
    volume_matrix,
    trace_turned,
    trace_matrix,
    lift_matrix,
    inverse,
    others,
    traces,
    beside,
    partial,
    arrived,
    load_sem,
    sending,
    inst_recv,
    spread,
    column,
    plane,
    relayed,
    frequency,
    handed,
    relay_recv,
):
    local, dof, elements = current.shape
    width = trace_matrix.shape[0] // 6
    iface = partner.shape[2]
    parts = split(local, elements)
    my_inst = lax.axis_index("inst")
    my_space = lax.axis_index("space")
    section = lax.axis_index("row")
    right = lax.rem(my_space + 1, shards)
    left = lax.rem(my_space + shards - 1, shards)

    barrier = pltpu.get_barrier_semaphore()
    def signal(semaphore, target):
        pl.semaphore_signal(semaphore, inc=1, device_id=target, device_id_type=MESH)

    leads = my_inst == 0
    other_row = {"row": 1 - section}
    peers = [{"inst": lax.rem(my_inst + k, insts)} for k in range(1, insts)]
    for peer in peers:
        signal(barrier, peer)

    @pl.when(leads)
    def _():
        signal(barrier, other_row)

    @pl.when(jnp.logical_and(leads, my_space < shards - 1))
    def _():
        signal(barrier, {"space": my_space + 1})

    greeted = jnp.where(leads, 1 + jnp.minimum(my_space, 1), 0)
    pl.semaphore_wait(barrier, insts - 1 + greeted)

    early = range(1, 2 + min(local - 1, 1))
    late = range(early.stop, len(parts))

    def inst_copy(k, part):
        picked, start, stop = parts[part]
        return pltpu.make_async_remote_copy(
            src_ref=solution_hbm.at[0, picked, :, start:stop],
            dst_ref=others.at[k - 1, picked, :, start:stop],
            send_sem=sending,
            recv_sem=inst_recv.at[k - 1, max(part - early.stop + 1, 0)],
            device_id={"inst": lax.rem(my_inst + k, insts)},
            device_id_type=MESH,
        )


    def send(numbers):
        for part in numbers:
            for k in range(1, insts):
                inst_copy(k, part).start()

    holds = jnp.logical_and(leads, section == 0)

    def share(k):
        return pltpu.make_async_remote_copy(
            src_ref=given,
            dst_ref=frequency,
            send_sem=sending,
            recv_sem=handed,
            device_id=peers[k - 1],
            device_id_type=MESH,
        )

    @pl.when(holds)
    def _():
        for k in range(1, insts):
            share(k).start()

    @pl.when(section == 0)
    def _():
        send(early)
        send(late)

    @pl.when(section == 1)
    def _():
        send(range(early.stop))

    final = len(parts) - 1

    def relay(part):
        picked, start, stop = parts[part]
        return pltpu.make_async_remote_copy(
            src_ref=solution_hbm.at[0, picked.start, :, start:stop],
            dst_ref=relayed,
            send_sem=sending,
            recv_sem=relay_recv,
            device_id=other_row,
            device_id_type=MESH,
        )

    def onward(k, part, row):
        picked, start, stop = parts[part]
        return pltpu.make_async_remote_copy(
            src_ref=relayed,
            dst_ref=others.at[k - 1, picked.start, :, start:stop],
            send_sem=sending,
            recv_sem=inst_recv.at[k - 1, max(part - early.stop + 1, 0)],
            device_id={"inst": lax.rem(my_inst + k, insts), "row": row},
            device_id_type=MESH,
        )

    loads = []
    for number, (source, target) in enumerate(
        (
            (trace_hbm, trace_turned),
            (solution_hbm.at[0], current),
            (volume_hbm, volume_matrix),
            (lift_hbm, lift_matrix),
            (forcing_hbm.at[0], forcing),
            (inverse_hbm, inverse),
            (adjacency_hbm, adjacency),
            (partner_hbm, partner),
            (scales_hbm, scales),
            (table_hbm, table),
        )
    ):
        copy = pltpu.make_async_copy(source, target, load_sem.at[min(number // 3, 1)])
        copy.start()
        loads.append(copy)

    @pl.when(jnp.logical_and(leads, my_space == shards - 1))
    def _():
        signal(column, {"space": my_space - 1})

    for copy in loads[:3]:
        copy.wait()
    trace_matrix[...] = trace_turned[...].T

    def trace_tile(t, carry):
        columns = pl.ds(pl.multiple_of(t * TILE, TILE), TILE)
        for n in range(local):
            values = mm(trace_matrix[...], current[n, :, columns]).astype(jnp.bfloat16)
            for f in range(6):
                traces[f, n * width : (n + 1) * width, columns] = values[
                    f * width : (f + 1) * width
                ]
        return carry

    lax.fori_loop(0, elements // TILE, trace_tile, 0)

    @pl.when(jnp.logical_and(leads, my_space < shards - 1))
    def _():
        pl.semaphore_wait(column, 1)

    @pl.when(jnp.logical_and(leads, jnp.logical_and(my_space > 0, my_space < shards - 1)))
    def _():
        signal(column, {"space": my_space - 1})

    @pl.when(jnp.logical_and(leads, my_space == 0))
    def _():
        for j in range(1, shards):
            signal(column, {"space": j})

    def volume_tile(t, carry):
        columns = pl.ds(pl.multiple_of(t * TILE, TILE), TILE)
        for n in range(local):
            partial[n, :, columns] = mm(volume_matrix[...], current[n, :, columns])
        return carry

    lax.fori_loop(0, elements // TILE, volume_tile, 0)

    @pl.when(jnp.logical_and(leads, my_space > 0))
    def _():
        pl.semaphore_wait(column, 1)

    @pl.when(leads)
    def _():
        signal(plane, other_row)
        pl.semaphore_wait(plane, 1)
        for peer in peers:
            signal(plane, peer)

    @pl.when(jnp.logical_not(leads))
    def _():
        pl.semaphore_wait(plane, 1)

    across = pltpu.make_async_remote_copy(
        src_ref=frequency,
        dst_ref=frequency,
        send_sem=sending,
        recv_sem=handed,
        device_id=other_row,
        device_id_type=MESH,
    )

    @pl.when(holds)
    def _():
        frequency[...] = given[...]

    if insts > 1:

        @pl.when(jnp.logical_and(jnp.logical_not(leads), section == 0))
        def _():
            share(1).wait_recv()

    @pl.when(section == 0)
    def _():
        across.start()
        relay(0).start()

    @pl.when(section == 1)
    def _():
        relay(final).start()

    to_left = pltpu.make_async_remote_copy(
        src_ref=traces.at[4:6, :, 0:LANES],
        dst_ref=arrived.at[2:4],
        send_sem=sending,
        recv_sem=spread,
        device_id={"space": left},
        device_id_type=MESH,
    )
    to_right = pltpu.make_async_remote_copy(
        src_ref=traces.at[4:6, :, elements - LANES : elements],
        dst_ref=arrived.at[0:2],
        send_sem=sending,
        recv_sem=spread,
        device_id={"space": right},
        device_id_type=MESH,
    )
    to_left.start()
    to_right.start()

    def cross_copy(j, slot):
        return pltpu.make_async_remote_copy(
            src_ref=traces.at[1 - section, :, 0:LANES],
            dst_ref=arrived.at[4 + slot],
            send_sem=sending,
            recv_sem=spread,
            device_id={"space": j, "row": 1 - section},
            device_id_type=MESH,
        )

    for j in range(shards):
        cross_copy(j, my_space).start()

    def put(face, columns, values):
        for n in range(local):
            beside[n, face * width : (face + 1) * width, columns] = values[
                n * width : (n + 1) * width
            ].astype(jnp.bfloat16)

    for copy in loads[3:]:
        copy.wait()
    for face in range(6):

        def gather_tile(t, carry, face=face):
            columns = pl.ds(pl.multiple_of(t * TILE, TILE), TILE)
            ids = adjacency[face, :, columns]
            put(face, columns, mm(traces[OPPOSITE[face]], one_hot(ids, LAYER, elements)))
            return carry

        lax.fori_loop(0, elements // TILE, gather_tile, 0)
        if face == 1:

            relay(0).wait_recv()

            @pl.when(section == 0)
            def _():
                for k in range(1, insts):
                    onward(k, final, 1).start()

            @pl.when(section == 1)
            def _():
                across.wait_recv()
                for k in range(1, insts):
                    onward(k, 0, 0).start()
                send(late[:-1])

    every = pltpu.make_async_remote_copy(
        src_ref=arrived,
        dst_ref=arrived,
        send_sem=sending,
        recv_sem=spread,
        device_id=other_row,
        device_id_type=MESH,
    )
    every.wait_recv()
    ends = (0,) if elements == LANES else (0, elements - LANES)
    for face in (4, 5):
        for start in ends:
            columns = pl.ds(start, LANES)
            ids = adjacency[face, :, columns]
            facing = OPPOSITE[face] - 4
            low = mm(arrived[facing], one_hot(ids, LAYER - LANES, LANES))
            high = mm(arrived[2 + facing], one_hot(ids, LAYER + elements, LANES))
            for n in range(local):
                rows = slice(face * width, (face + 1) * width)
                lines = slice(n * width, (n + 1) * width)
                beside[n, rows, columns] = (
                    beside[n, rows, columns].astype(jnp.float32) + low[lines] + high[lines]
                ).astype(jnp.bfloat16)

    for n in range(local):
        ids = partner[0, n : n + 1, :]
        lines = slice(n * width, (n + 1) * width)
        total = jnp.zeros((width, iface), jnp.float32)
        for j in range(shards):
            hot = one_hot(ids, j * iface, iface)
            total += mm(arrived[4 + j, lines, 0:iface], hot)
        incoming = total.astype(jnp.bfloat16)
        for face in range(2):
            rows = slice(face * width, (face + 1) * width)
            beside[n, rows, 0:iface] = jnp.where(
                section == 1 - face, incoming, beside[n, rows, 0:iface]
            )


    factor = frequency[0:1, 0:1]
    all_inst = local * insts

    def weight(n, owner, m):
        return factor * table[(my_inst * local + n) * all_inst + owner * local + m]

    def lift_tile(t, carry):
        columns = pl.ds(pl.multiple_of(t * TILE, TILE), TILE)
        scale = scales[:, columns]
        inverse_scale = 1.0 / scale
        for n in range(local):
            coupled = mm(lift_matrix[...], beside[n, :, columns])
            residual = forcing[n, :, columns].astype(jnp.float32) - scale * (
                partial[n, :, columns] + coupled
            )
            for m in range(local):
                residual -= weight(n, my_inst, m) * current[m, :, columns].astype(jnp.float32)
            update = mm(inverse[...], residual.astype(jnp.bfloat16))
            partial[n, :, columns] = (
                current[n, :, columns].astype(jnp.float32) + update * inverse_scale
            )
        return carry

    lax.fori_loop(0, elements // TILE, lift_tile, 0)

    def first_half(k):
        block = others.at[k - 1, :, :, 0 : parts[early.stop][1]]
        return pltpu.make_async_remote_copy(
            src_ref=block,
            dst_ref=block,
            send_sem=sending,
            recv_sem=inst_recv.at[k - 1, 0],
            device_id=peers[k - 1],
            device_id_type=MESH,
        )

    for part, (picked, start, stop) in enumerate(parts):
        chosen = range(local)[picked]
        wide = TILE if (stop - start) % TILE == 0 else CHUNK
        for k in range(1, insts):
            owner = lax.rem(my_inst + insts - k, insts)
            last = k == insts - 1 and chosen[-1] == local - 1
            if part == 0:
                first_half(k).wait_recv()
            elif part >= early.stop:
                inst_copy(k, part).wait_recv()

            def turn_tile(t, carry):
                columns = pl.ds(pl.multiple_of(start + t * wide, wide), wide)
                inverse_scale = 1.0 / scales[:, columns]
                values = [partial[n, :, columns] for n in range(local)]
                for m in chosen:
                    update = mm(inverse[...], others[k - 1, m, :, columns]) * inverse_scale
                    values = [values[n] - weight(n, owner, m) * update for n in range(local)]
                for n in range(local):
                    if last:
                        result[0, n, :, columns] = values[n].astype(jnp.bfloat16)
                    else:
                        partial[n, :, columns] = values[n]
                return carry

            lax.fori_loop(0, (stop - start) // wide, turn_tile, 0)

    if insts == 1:
        result[0] = partial[...].astype(jnp.bfloat16)

    every.wait_send()

    def sent(source):
        pltpu.make_async_remote_copy(
            src_ref=source,
            dst_ref=source,
            send_sem=sending,
            recv_sem=handed,
            device_id=other_row,
            device_id_type=MESH,
        ).wait_send()

    @pl.when(holds)
    def _():
        for _ in peers:
            sent(frequency)

    @pl.when(section == 0)
    def _():
        sent(frequency)

    sent(relayed)
    sent(others)


def split(local, elements):
    half = elements // (2 * CHUNK) * CHUNK
    parts = [(slice(0, 1), 0, CHUNK), (slice(0, 1), CHUNK, half)]
    if local > 1:
        parts.append((slice(1, local), 0, half))
    start = half
    if elements - start > CHUNK:
        parts.append((slice(0, local), start, elements - CHUNK))
        start = elements - CHUNK
    return parts + [(slice(m, m + 1), start, elements) for m in range(local)]


def body(
    solution,
    forcing,
    metric_scale,
    frequency,
    adjacency,
    partner,
    volume_matrix,
    trace_matrix,
    lift_matrix,
    block_inverse,
):
    insts = lax.axis_size("inst")
    shards = lax.axis_size("space")
    _, local, dof, elements = solution.shape
    width = trace_matrix.shape[0] // 6
    parts = split(local, elements)
    table = jnp.asarray(spectral_constants(local * insts).reshape(-1))
    vmem = pl.BlockSpec(memory_space=pltpu.VMEM)
    away = pl.BlockSpec(memory_space=pltpu.HBM)
    narrow = jnp.bfloat16
    grant = 67043328 - 2 * solution.size - 65536
    dma = pltpu.SemaphoreType.DMA
    return pl.pallas_call(
        functools.partial(kernel, insts, shards),
        name="sweep",
        out_shape=pltpu.VMEM(solution.shape, narrow),
        in_specs=[vmem] + [away] * 10,
        out_specs=vmem,
        scratch_shapes=[
            pltpu.SMEM(table.shape, jnp.float32),
            pltpu.VMEM(metric_scale.shape, jnp.float32),
            pltpu.VMEM((6, 1, elements), jnp.int32),
            pltpu.VMEM(partner.shape, jnp.int32),
            pltpu.VMEM((local, dof, elements), narrow),
            pltpu.VMEM((local, dof, elements), narrow),
            pltpu.VMEM(volume_matrix.shape, narrow),
            pltpu.VMEM(trace_matrix.shape[::-1], narrow),
            pltpu.VMEM(trace_matrix.shape, narrow),
            pltpu.VMEM(lift_matrix.shape, narrow),
            pltpu.VMEM(block_inverse.shape, narrow),
            pltpu.VMEM((max(insts - 1, 1), local, dof, elements), narrow),
            pltpu.VMEM((6, local * width, elements), narrow),
            pltpu.VMEM((local, 6 * width, elements), narrow),
            pltpu.VMEM((local, dof, elements), jnp.float32),
            pltpu.VMEM((4 + shards, local * width, LANES), narrow),
            dma((2,)),
            dma,
            dma((max(insts - 1, 1), len(parts) - min(local - 1, 1) - 1)),
            dma,
            pltpu.SemaphoreType.REGULAR,
            pltpu.SemaphoreType.REGULAR,
            pltpu.VMEM((dof, CHUNK), narrow),
            pltpu.VMEM((8, LANES), jnp.float32),
            dma,
            dma,
        ],
        compiler_params=pltpu.CompilerParams(
            collective_id=0, has_side_effects=True, vmem_limit_bytes=grant
        ),
    )(
        lax.cond(
            jnp.logical_and(lax.axis_index("inst") == 0, lax.axis_index("row") == 0),
            lambda value: jnp.broadcast_to(value, (8, LANES)),
            lambda value: jnp.zeros((8, LANES), jnp.float32),
            frequency,
        ),
        table,
        metric_scale,
        jnp.transpose(adjacency, (1, 0, 2)),
        partner,
        solution,
        forcing,
        volume_matrix,
        trace_matrix.T,
        lift_matrix,
        block_inverse,
    )


def solution(mesh):
    in_specs = (
        P("row", "inst", None, ("groups", "space")),
        P("row", "inst", None, ("groups", "space")),
        P("row", ("groups", "space")),
        P(),
        P("row", None, ("groups", "space")),
        P("row", "inst", ("groups", "space")),
        P(),
        P(),
        P(),
        P(),
    )
    out_specs = P("row", "inst", None, ("groups", "space"))
    return jax.shard_map(body, mesh=mesh, in_specs=in_specs, out_specs=out_specs, check_vma=False)
```

```python
import functools

import jax
import jax.numpy as jnp
import numpy as np
from jax import lax
from jax.experimental import pallas as pl
from jax.experimental.pallas import tpu as pltpu
from jax.sharding import PartitionSpec as P

LAYER = 64
LANES = 128
CHUNK = 128
TILE = 256
OPPOSITE = (1, 0, 3, 2, 5, 4)
MESH = pl.DeviceIdType.MESH


def spectral_constants(instances):
    positions = np.arange(instances)
    distance = (positions[:, None] - positions[None, :]).astype(np.float32)
    parity = (1.0 - 2.0 * np.mod(positions[:, None] + positions[None, :], 2)).astype(np.float32)
    angles = (np.float32(np.pi) * distance / np.float32(instances)).astype(np.float32)
    sine_values = np.where(distance == 0.0, np.float32(1.0), np.sin(angles))
    cotangent = np.where(distance == 0.0, np.float32(0.0), np.cos(angles) / sine_values)
    return (np.float32(0.5) * parity * cotangent).astype(np.float32)


def one_hot(ids, first, rows):
    numbers = lax.broadcasted_iota(jnp.int32, (rows, ids.shape[1]), 0) + first
    return jnp.where(numbers == ids, 1.0, 0.0).astype(jnp.bfloat16)


def mm(a, b):
    return jnp.dot(a, b, preferred_element_type=jnp.float32)


def kernel(
    insts,
    shards,
    given,
    table_hbm,
    scales_hbm,
    adjacency_hbm,
    partner_hbm,
    solution_hbm,
    forcing_hbm,
    volume_hbm,
    trace_hbm,
    lift_hbm,
    inverse_hbm,
    result,
    table,
    scales,
    adjacency,
    partner,
    current,
    forcing,
    volume_matrix,
    trace_turned,
    trace_matrix,
    lift_matrix,
    inverse,
    others,
    traces,
    beside,
    partial,
    arrived,
    load_sem,
    sending,
    inst_recv,
    spread,
    column,
    plane,
    relayed,
    frequency,
    handed,
    relay_recv,
):
    local, dof, elements = current.shape
    width = trace_matrix.shape[0] // 6
    iface = partner.shape[2]
    parts = split(local, elements)
    my_inst = lax.axis_index("inst")
    my_space = lax.axis_index("space")
    section = lax.axis_index("row")
    right = lax.rem(my_space + 1, shards)
    left = lax.rem(my_space + shards - 1, shards)

    barrier = pltpu.get_barrier_semaphore()
    def signal(semaphore, target):
        pl.semaphore_signal(semaphore, inc=1, device_id=target, device_id_type=MESH)

    leads = my_inst == 0
    other_row = {"row": 1 - section}
    peers = [{"inst": lax.rem(my_inst + k, insts)} for k in range(1, insts)]
    for peer in peers:
        signal(barrier, peer)

    @pl.when(leads)
    def _():
        signal(barrier, other_row)

    @pl.when(jnp.logical_and(leads, my_space < shards - 1))
    def _():
        signal(barrier, {"space": my_space + 1})

    greeted = jnp.where(leads, 1 + jnp.minimum(my_space, 1), 0)
    pl.semaphore_wait(barrier, insts - 1 + greeted)

    early = range(1, 2 + min(local - 1, 1))
    late = range(early.stop, len(parts))

    def inst_copy(k, part):
        picked, start, stop = parts[part]
        return pltpu.make_async_remote_copy(
            src_ref=solution_hbm.at[0, picked, :, start:stop],
            dst_ref=others.at[k - 1, picked, :, start:stop],
            send_sem=sending,
            recv_sem=inst_recv.at[k - 1, max(part - early.stop + 1, 0)],
            device_id={"inst": lax.rem(my_inst + k, insts)},
            device_id_type=MESH,
        )


    def send(numbers):
        for part in numbers:
            for k in range(1, insts):
                inst_copy(k, part).start()

    holds = jnp.logical_and(leads, section == 0)

    def share(k):
        return pltpu.make_async_remote_copy(
            src_ref=given,
            dst_ref=frequency,
            send_sem=sending,
            recv_sem=handed,
            device_id=peers[k - 1],
            device_id_type=MESH,
        )

    @pl.when(holds)
    def _():
        for k in range(1, insts):
            share(k).start()

    @pl.when(section == 0)
    def _():
        send(early)
        send(late)

    @pl.when(section == 1)
    def _():
        columns = slice(0, parts[early.stop][1])
        for k in range(1, insts):
            pltpu.make_async_remote_copy(
                src_ref=solution_hbm.at[0, :, :, columns],
                dst_ref=others.at[k - 1, :, :, columns],
                send_sem=sending,
                recv_sem=inst_recv.at[k - 1, 0],
                device_id=peers[k - 1],
                device_id_type=MESH,
            ).start()

    final = len(parts) - 1

    def relay(part):
        picked, start, stop = parts[part]
        return pltpu.make_async_remote_copy(
            src_ref=solution_hbm.at[0, picked.start, :, start:stop],
            dst_ref=relayed,
            send_sem=sending,
            recv_sem=relay_recv,
            device_id=other_row,
            device_id_type=MESH,
        )

    def onward(k, part, row):
        picked, start, stop = parts[part]
        return pltpu.make_async_remote_copy(
            src_ref=relayed,
            dst_ref=others.at[k - 1, picked.start, :, start:stop],
            send_sem=sending,
            recv_sem=inst_recv.at[k - 1, max(part - early.stop + 1, 0)],
            device_id={"inst": lax.rem(my_inst + k, insts), "row": row},
            device_id_type=MESH,
        )

    loads = []
    for number, (source, target) in enumerate(
        (
            (trace_hbm, trace_turned),
            (solution_hbm.at[0], current),
            (volume_hbm, volume_matrix),
            (lift_hbm, lift_matrix),
            (forcing_hbm.at[0], forcing),
            (inverse_hbm, inverse),
            (adjacency_hbm, adjacency),
            (partner_hbm, partner),
            (scales_hbm, scales),
            (table_hbm, table),
        )
    ):
        copy = pltpu.make_async_copy(source, target, load_sem.at[min(number // 3, 1)])
        copy.start()
        loads.append(copy)

    @pl.when(jnp.logical_and(leads, my_space == shards - 1))
    def _():
        signal(column, {"space": my_space - 1})

    for copy in loads[:3]:
        copy.wait()
    trace_matrix[...] = trace_turned[...].T

    def trace_tile(t, carry):
        columns = pl.ds(pl.multiple_of(t * TILE, TILE), TILE)
        for n in range(local):
            values = mm(trace_matrix[...], current[n, :, columns]).astype(jnp.bfloat16)
            for f in range(6):
                traces[f, n * width : (n + 1) * width, columns] = values[
                    f * width : (f + 1) * width
                ]
        return carry

    lax.fori_loop(0, elements // TILE, trace_tile, 0)

    @pl.when(jnp.logical_and(leads, my_space < shards - 1))
    def _():
        pl.semaphore_wait(column, 1)

    @pl.when(jnp.logical_and(leads, jnp.logical_and(my_space > 0, my_space < shards - 1)))
    def _():
        signal(column, {"space": my_space - 1})

    @pl.when(jnp.logical_and(leads, my_space == 0))
    def _():
        for j in range(1, shards):
            signal(column, {"space": j})

    def volume_tile(t, carry):
        columns = pl.ds(pl.multiple_of(t * TILE, TILE), TILE)
        for n in range(local):
            partial[n, :, columns] = mm(volume_matrix[...], current[n, :, columns])
        return carry

    lax.fori_loop(0, elements // TILE, volume_tile, 0)

    @pl.when(jnp.logical_and(leads, my_space > 0))
    def _():
        pl.semaphore_wait(column, 1)

    @pl.when(leads)
    def _():
        signal(plane, other_row)
        pl.semaphore_wait(plane, 1)
        for peer in peers:
            signal(plane, peer)

    @pl.when(jnp.logical_not(leads))
    def _():
        pl.semaphore_wait(plane, 1)

    across = pltpu.make_async_remote_copy(
        src_ref=frequency,
        dst_ref=frequency,
        send_sem=sending,
        recv_sem=handed,
        device_id=other_row,
        device_id_type=MESH,
    )

    @pl.when(holds)
    def _():
        frequency[...] = given[...]

    if insts > 1:

        @pl.when(jnp.logical_and(jnp.logical_not(leads), section == 0))
        def _():
            share(1).wait_recv()

    @pl.when(section == 0)
    def _():
        across.start()
        relay(0).start()

    @pl.when(section == 1)
    def _():
        relay(final).start()

    to_left = pltpu.make_async_remote_copy(
        src_ref=traces.at[4:6, :, 0:LANES],
        dst_ref=arrived.at[2:4],
        send_sem=sending,
        recv_sem=spread,
        device_id={"space": left},
        device_id_type=MESH,
    )
    to_right = pltpu.make_async_remote_copy(
        src_ref=traces.at[4:6, :, elements - LANES : elements],
        dst_ref=arrived.at[0:2],
        send_sem=sending,
        recv_sem=spread,
        device_id={"space": right},
        device_id_type=MESH,
    )
    to_left.start()
    to_right.start()

    def cross_copy(j, slot):
        return pltpu.make_async_remote_copy(
            src_ref=traces.at[1 - section, :, 0:LANES],
            dst_ref=arrived.at[4 + slot],
            send_sem=sending,
            recv_sem=spread,
            device_id={"space": j, "row": 1 - section},
            device_id_type=MESH,
        )

    for j in range(shards):
        cross_copy(j, my_space).start()

    def put(face, columns, values):
        for n in range(local):
            beside[n, face * width : (face + 1) * width, columns] = values[
                n * width : (n + 1) * width
            ].astype(jnp.bfloat16)

    for copy in loads[3:]:
        copy.wait()
    for face in range(6):

        def gather_tile(t, carry, face=face):
            columns = pl.ds(pl.multiple_of(t * TILE, TILE), TILE)
            ids = adjacency[face, :, columns]
            put(face, columns, mm(traces[OPPOSITE[face]], one_hot(ids, LAYER, elements)))
            return carry

        lax.fori_loop(0, elements // TILE, gather_tile, 0)
        if face == 1:

            relay(0).wait_recv()

            @pl.when(section == 0)
            def _():
                for k in range(1, insts):
                    onward(k, final, 1).start()

            @pl.when(section == 1)
            def _():
                across.wait_recv()
                for k in range(1, insts):
                    onward(k, 0, 0).start()
                send(late[:-1])

    every = pltpu.make_async_remote_copy(
        src_ref=arrived,
        dst_ref=arrived,
        send_sem=sending,
        recv_sem=spread,
        device_id=other_row,
        device_id_type=MESH,
    )
    every.wait_recv()
    ends = (0,) if elements == LANES else (0, elements - LANES)
    for face in (4, 5):
        for start in ends:
            columns = pl.ds(start, LANES)
            ids = adjacency[face, :, columns]
            facing = OPPOSITE[face] - 4
            low = mm(arrived[facing], one_hot(ids, LAYER - LANES, LANES))
            high = mm(arrived[2 + facing], one_hot(ids, LAYER + elements, LANES))
            for n in range(local):
                rows = slice(face * width, (face + 1) * width)
                lines = slice(n * width, (n + 1) * width)
                beside[n, rows, columns] = (
                    beside[n, rows, columns].astype(jnp.float32) + low[lines] + high[lines]
                ).astype(jnp.bfloat16)

    for n in range(local):
        ids = partner[0, n : n + 1, :]
        lines = slice(n * width, (n + 1) * width)
        total = jnp.zeros((width, iface), jnp.float32)
        for j in range(shards):
            hot = one_hot(ids, j * iface, iface)
            total += mm(arrived[4 + j, lines, 0:iface], hot)
        incoming = total.astype(jnp.bfloat16)
        for face in range(2):
            rows = slice(face * width, (face + 1) * width)
            beside[n, rows, 0:iface] = jnp.where(
                section == 1 - face, incoming, beside[n, rows, 0:iface]
            )


    factor = frequency[0:1, 0:1]
    all_inst = local * insts

    def weight(n, owner, m):
        return factor * table[(my_inst * local + n) * all_inst + owner * local + m]

    def lift_tile(t, carry):
        columns = pl.ds(pl.multiple_of(t * TILE, TILE), TILE)
        scale = scales[:, columns]
        inverse_scale = 1.0 / scale
        for n in range(local):
            coupled = mm(lift_matrix[...], beside[n, :, columns])
            residual = forcing[n, :, columns].astype(jnp.float32) - scale * (
                partial[n, :, columns] + coupled
            )
            for m in range(local):
                residual -= weight(n, my_inst, m) * current[m, :, columns].astype(jnp.float32)
            update = mm(inverse[...], residual.astype(jnp.bfloat16))
            partial[n, :, columns] = (
                current[n, :, columns].astype(jnp.float32) + update * inverse_scale
            )
        return carry

    lax.fori_loop(0, elements // TILE, lift_tile, 0)

    def first_half(k):
        block = others.at[k - 1, :, :, 0 : parts[early.stop][1]]
        return pltpu.make_async_remote_copy(
            src_ref=block,
            dst_ref=block,
            send_sem=sending,
            recv_sem=inst_recv.at[k - 1, 0],
            device_id=peers[k - 1],
            device_id_type=MESH,
        )

    for part, (picked, start, stop) in enumerate(parts):
        chosen = range(local)[picked]
        wide = TILE if (stop - start) % TILE == 0 else CHUNK
        for k in range(1, insts):
            owner = lax.rem(my_inst + insts - k, insts)
            last = k == insts - 1 and chosen[-1] == local - 1
            if part == 0:
                first_half(k).wait_recv()
            elif part >= early.stop:
                inst_copy(k, part).wait_recv()

            def turn_tile(t, carry):
                columns = pl.ds(pl.multiple_of(start + t * wide, wide), wide)
                inverse_scale = 1.0 / scales[:, columns]
                values = [partial[n, :, columns] for n in range(local)]
                for m in chosen:
                    update = mm(inverse[...], others[k - 1, m, :, columns]) * inverse_scale
                    values = [values[n] - weight(n, owner, m) * update for n in range(local)]
                for n in range(local):
                    if last:
                        result[0, n, :, columns] = values[n].astype(jnp.bfloat16)
                    else:
                        partial[n, :, columns] = values[n]
                return carry

            lax.fori_loop(0, (stop - start) // wide, turn_tile, 0)

    if insts == 1:
        result[0] = partial[...].astype(jnp.bfloat16)

    every.wait_send()

    def sent(source):
        pltpu.make_async_remote_copy(
            src_ref=source,
            dst_ref=source,
            send_sem=sending,
            recv_sem=handed,
            device_id=other_row,
            device_id_type=MESH,
        ).wait_send()

    @pl.when(holds)
    def _():
        for _ in peers:
            sent(frequency)

    @pl.when(section == 0)
    def _():
        sent(frequency)

    sent(relayed)
    sent(others)


def split(local, elements):
    half = elements // (2 * CHUNK) * CHUNK
    parts = [(slice(0, 1), 0, CHUNK), (slice(0, 1), CHUNK, half)]
    if local > 1:
        parts.append((slice(1, local), 0, half))
    start = half
    if elements - start > CHUNK:
        parts.append((slice(0, local), start, elements - CHUNK))
        start = elements - CHUNK
    return parts + [(slice(m, m + 1), start, elements) for m in range(local)]


def body(
    solution,
    forcing,
    metric_scale,
    frequency,
    adjacency,
    partner,
    volume_matrix,
    trace_matrix,
    lift_matrix,
    block_inverse,
):
    insts = lax.axis_size("inst")
    shards = lax.axis_size("space")
    _, local, dof, elements = solution.shape
    width = trace_matrix.shape[0] // 6
    parts = split(local, elements)
    table = jnp.asarray(spectral_constants(local * insts).reshape(-1))
    vmem = pl.BlockSpec(memory_space=pltpu.VMEM)
    away = pl.BlockSpec(memory_space=pltpu.HBM)
    narrow = jnp.bfloat16
    grant = 67043328 - 2 * solution.size - 65536
    dma = pltpu.SemaphoreType.DMA
    return pl.pallas_call(
        functools.partial(kernel, insts, shards),
        name="sweep",
        out_shape=pltpu.VMEM(solution.shape, narrow),
        in_specs=[vmem] + [away] * 10,
        out_specs=vmem,
        scratch_shapes=[
            pltpu.SMEM(table.shape, jnp.float32),
            pltpu.VMEM(metric_scale.shape, jnp.float32),
            pltpu.VMEM((6, 1, elements), jnp.int32),
            pltpu.VMEM(partner.shape, jnp.int32),
            pltpu.VMEM((local, dof, elements), narrow),
            pltpu.VMEM((local, dof, elements), narrow),
            pltpu.VMEM(volume_matrix.shape, narrow),
            pltpu.VMEM(trace_matrix.shape[::-1], narrow),
            pltpu.VMEM(trace_matrix.shape, narrow),
            pltpu.VMEM(lift_matrix.shape, narrow),
            pltpu.VMEM(block_inverse.shape, narrow),
            pltpu.VMEM((max(insts - 1, 1), local, dof, elements), narrow),
            pltpu.VMEM((6, local * width, elements), narrow),
            pltpu.VMEM((local, 6 * width, elements), narrow),
            pltpu.VMEM((local, dof, elements), jnp.float32),
            pltpu.VMEM((4 + shards, local * width, LANES), narrow),
            dma((2,)),
            dma,
            dma((max(insts - 1, 1), len(parts) - min(local - 1, 1) - 1)),
            dma,
            pltpu.SemaphoreType.REGULAR,
            pltpu.SemaphoreType.REGULAR,
            pltpu.VMEM((dof, CHUNK), narrow),
            pltpu.VMEM((8, LANES), jnp.float32),
            dma,
            dma,
        ],
        compiler_params=pltpu.CompilerParams(
            collective_id=0, has_side_effects=True, vmem_limit_bytes=grant
        ),
    )(
        lax.cond(
            jnp.logical_and(lax.axis_index("inst") == 0, lax.axis_index("row") == 0),
            lambda value: jnp.broadcast_to(value, (8, LANES)),
            lambda value: jnp.zeros((8, LANES), jnp.float32),
            frequency,
        ),
        table,
        metric_scale,
        jnp.transpose(adjacency, (1, 0, 2)),
        partner,
        solution,
        forcing,
        volume_matrix,
        trace_matrix.T,
        lift_matrix,
        block_inverse,
    )


def solution(mesh):
    in_specs = (
        P("row", "inst", None, ("groups", "space")),
        P("row", "inst", None, ("groups", "space")),
        P("row", ("groups", "space")),
        P(),
        P("row", None, ("groups", "space")),
        P("row", "inst", ("groups", "space")),
        P(),
        P(),
        P(),
        P(),
    )
    out_specs = P("row", "inst", None, ("groups", "space"))
    return jax.shard_map(body, mesh=mesh, in_specs=in_specs, out_specs=out_specs, check_vma=False)
```
